512 devices in a mesh: ctx: 16 (over y, core), chan: 32 (over z, x).
Axes of the slice: x: 4, y: 8, z: 8, core: 2. Of those that a mesh axis runs over, the one named last changes fastest.
Arguments:
- out_gate: bfloat16 [512, 16384], P('chan', 'ctx'), may hold values from -6 to 6
- in_gate: bfloat16 [512, 16384], P('chan', 'ctx'), may hold values from -6 to 6
- signal: bfloat16 [512, 16384], P('chan', 'ctx'), may hold values from -6 to 6
- grad_out: bfloat16 [512, 16384], P('chan', 'ctx'), may hold values from -6 to 6
- position_table: float32 [33, 16384], P(None, 'ctx'), may hold values from -6 to 6
- embed_weight: float32 [33, 64], replicated, may hold values from -1 to 1
- hidden_weight: float32 [64, 64], replicated, may hold values from -0.75 to 0.75
- filter_weight: float32 [64, 512], P(None, 'chan'), may hold values from -0.75 to 0.75
- decay_rate: float32 [512], P('chan'), may hold values from 0 to 1, as said below
- skip_gain: float32 [512], P('chan'), may hold values from -6 to 6
Outputs:
- mixed: bfloat16 [512, 16384], P('chan', 'ctx')
- out_gate_grad: bfloat16 [512, 16384], P('chan', 'ctx')
- in_gate_grad: bfloat16 [512, 16384], P('chan', 'ctx')
- signal_grad: bfloat16 [512, 16384], P('chan', 'ctx')
- embed_weight_grad: float32 [33, 64], replicated
- hidden_weight_grad: float32 [64, 64], replicated
- filter_weight_grad: float32 [64, 512], P(None, 'chan')
- skip_gain_grad: float32 [512], P('chan')
- position_grad: float32 [33, 16384], P(None, 'ctx')
The draws below stay inside these ranges and needn't reach their ends.
Inputs may be any that keep to these rules, and one draw needn't show every extreme that they name: `decay_rate`: positive decay rates; some channels keep their filter over the whole sequence, the others decay with e-fold lengths from about 30 positions to a large fraction of the sequence.
All inputs are finite; a program needn't handle non-finite values.
Results may differ from the reference program's by a relative error of at most 0.0013.
Values sent between devices are 32-bit elements; how exact they have to be, the bound alone decides.
A program may use at most 64 MiB of HBM per device.

```python
import math
import jax
import jax.numpy as jnp
from jax import lax

D = 512
E = 33
F = 64
SEQ = 16384


def draw_decay_rate(key, part):
    pick_key = jax.random.fold_in(key, 11)
    slow_key = jax.random.fold_in(key, 12)
    fast_key = jax.random.fold_in(key, 13)
    slow_share = 0.5
    picks = jax.random.uniform(pick_key, (D,), jnp.float32)
    slow_rates = jnp.exp(jax.random.uniform(slow_key, (D,), jnp.float32, math.log(0.2 / SEQ), math.log(2.0 / SEQ)))
    fast_rates = jnp.exp(jax.random.uniform(fast_key, (D,), jnp.float32, math.log(2.0 / SEQ), math.log(max(1.0 / 30.0, 4.0 / SEQ))))
    return jnp.where(picks < slow_share, slow_rates, fast_rates)


def level_of(rng, shape, split, smallest, high):
    def one(position, shards_of):
        heights = jax.random.uniform(jax.random.fold_in(jax.random.fold_in(rng, 6), position), (shards_of,), jnp.float32, smallest / len(split), high / len(split))
        return jnp.repeat(jnp.exp(heights), shape[position] // shards_of).reshape((-1,) + (1,) * (len(shape) - position - 1))

    level = one(*split[0])
    for cut in split[1:]:
        level = level * one(*cut)
    return level


def bell_draw(key, shape, deviation, reach, pieces=(), kind=jnp.bfloat16):
    result = jax.random.normal(key, shape, jnp.float32) * deviation
    if len(pieces) > 0:
        result = level_of(key, shape, pieces, -0.22, 0.18) * result
    return jnp.clip(result, min=-reach, max=reach).astype(kind)


def setup_inputs(seed: int = 0) -> dict:
    streams_of = jax.random.split(jax.random.key(seed), 11)
    return {
        "out_gate": bell_draw(streams_of[0], (D, SEQ), 1.0, 6.0, ((0, 32), (1, 16))),
        "in_gate": bell_draw(streams_of[1], (D, SEQ), 1.0, 6.0, ((0, 32), (1, 16))),
        "signal": bell_draw(streams_of[2], (D, SEQ), 1.0, 6.0, ((0, 32), (1, 16))),
        "grad_out": bell_draw(streams_of[3], (D, SEQ), 1.0, 6.0, ((0, 32), (1, 16))),
        "position_table": bell_draw(streams_of[4], (E, SEQ), 1.0, 6.0, ((1, 16),), jnp.float32),
        "embed_weight": bell_draw(streams_of[5], (E, F), E ** -0.5, 1.0, (), jnp.float32),
        "hidden_weight": bell_draw(streams_of[6], (F, F), F ** -0.5, 0.75, (), jnp.float32),
        "filter_weight": bell_draw(streams_of[7], (F, D), F ** -0.5, 0.75, ((1, 32),), jnp.float32),
        "decay_rate": draw_decay_rate(jax.random.fold_in(streams_of[10], 71), 0),
        "skip_gain": bell_draw(streams_of[9], (D,), 1.0, 6.0, ((0, 32),), jnp.float32),
    }


EPSILON = 1e-06

def matmul(left_side, right_side):
    return jnp.dot(left_side, right_side, precision=lax.Precision.HIGHEST, preferred_element_type=jnp.float32)

def spectrum(values):
    return jnp.fft.rfft(values, n=2 * SEQ, axis=-1)

def back_space(spectra):
    return jnp.fft.irfft(spectra, n=2 * SEQ, axis=-1)[:, :SEQ]

def reference(out_gate, in_gate, signal, grad_out, position_table, embed_weight, hidden_weight, filter_weight, decay_rate, skip_gain):
    pre_one = matmul(embed_weight.T, position_table)
    act_one = jnp.sin(pre_one)
    pre_two = matmul(hidden_weight.T, act_one)
    act_two = jnp.sin(pre_two)
    raw_filter = matmul(filter_weight.T, act_two)
    positions = jnp.arange(SEQ).astype(jnp.float32)
    envelope = jnp.exp(-decay_rate[:, None] * positions[None, :])
    shaped = raw_filter * envelope
    energy = lax.optimization_barrier(jnp.sum(shaped * shaped, axis=1))
    inverse_norm = lax.rsqrt(energy + EPSILON)
    kernel = shaped * inverse_norm[:, None]
    product = in_gate.astype(jnp.float32) * signal.astype(jnp.float32)
    kernel_spec = spectrum(kernel)
    product_spec = spectrum(product)
    conv = back_space(kernel_spec * product_spec)
    inner = conv + skip_gain[:, None] * product
    mixed = (out_gate.astype(jnp.float32) * inner).astype(jnp.bfloat16)
    upstream = grad_out.astype(jnp.float32)
    out_gate_grad = (upstream * inner).astype(jnp.bfloat16)
    through = upstream * out_gate.astype(jnp.float32)
    through_spec = spectrum(through)
    product_grad = back_space(jnp.conj(kernel_spec) * through_spec) + skip_gain[:, None] * through
    in_gate_grad = (product_grad * signal.astype(jnp.float32)).astype(jnp.bfloat16)
    signal_grad = (product_grad * in_gate.astype(jnp.float32)).astype(jnp.bfloat16)
    kernel_grad = back_space(jnp.conj(product_spec) * through_spec)
    along_kernel = lax.optimization_barrier(jnp.sum(kernel_grad * kernel, axis=1))
    raw_grad = (kernel_grad - kernel * along_kernel[:, None]) * inverse_norm[:, None] * envelope
    grad_scale = SEQ ** (-0.5)
    filter_weight_grad = matmul(act_two, raw_grad.T) * grad_scale
    act_two_grad = matmul(filter_weight, raw_grad)
    pre_two_grad = act_two_grad * jnp.cos(pre_two)
    hidden_weight_grad = matmul(act_one, pre_two_grad.T) * grad_scale
    act_one_grad = matmul(hidden_weight, pre_two_grad)
    pre_one_grad = act_one_grad * jnp.cos(pre_one)
    embed_weight_grad = matmul(position_table, pre_one_grad.T) * grad_scale
    position_grad = matmul(embed_weight, pre_one_grad)
    skip_gain_grad = lax.optimization_barrier(jnp.sum(through * product, axis=1)) * grad_scale
    return (mixed, out_gate_grad, in_gate_grad, signal_grad, embed_weight_grad, hidden_weight_grad, filter_weight_grad, skip_gain_grad, position_grad)
```

```python
import functools
import math

import jax
import jax.numpy as jnp
import ml_dtypes
import numpy as np
from jax import lax
from jax.experimental import pallas as pl
from jax.experimental.pallas import tpu as pltpu
from jax.sharding import PartitionSpec as P

EPSILON = 1e-06
F32 = jnp.float32
BF16 = jnp.bfloat16
LANES = 128
X_CHIPS = 4
PI_HIGH = 3.140625
PI_MID = 9.67502593994140625e-4
PI_LOW = 1.509957990978376432e-7


def halves(table):
    high = table.astype(ml_dtypes.bfloat16)
    low = (table - high.astype(np.float64)).astype(ml_dtypes.bfloat16)
    return np.stack([high, low])


@functools.lru_cache(maxsize=None)
def tables(row_count):
    total = 2 * row_count * LANES
    ids = np.arange(row_count)
    lane_ids = np.arange(LANES)
    angle = 2 * np.pi * np.outer(ids + 0.5, ids) / (2 * row_count)
    first = np.concatenate([np.cos(angle), -np.sin(angle)], axis=0)
    last = first.T * (2.0 / total)
    lane_angle = 2 * np.pi * np.outer(lane_ids, lane_ids) / LANES
    cosine, sine = np.cos(lane_angle), np.sin(lane_angle)
    second = np.block([[cosine, -sine], [sine, cosine]])
    twist_angle = 2 * np.pi * np.outer(ids + 0.5, lane_ids) / total
    twist = np.stack([np.cos(twist_angle), np.sin(twist_angle)]).astype(np.float32)
    return halves(first), halves(last), halves(second), halves(second.T), twist


def exact_dot(left, right, left_dim, right_dim):
    return lax.dot_general(
        left,
        right,
        (((left_dim,), (right_dim,)), ((), ())),
        precision=lax.Precision.HIGHEST,
        preferred_element_type=F32,
    )


def split(value):
    high = value.astype(BF16)
    return high, (value - high.astype(F32)).astype(BF16)


def plain_dot(left, right):
    return jnp.dot(left, right, preferred_element_type=F32)


def table_left(table, value):
    high, low = split(value)
    return plain_dot(table[0], high) + (plain_dot(table[0], low) + plain_dot(table[1], high))


def table_right(value, table):
    high, low = split(value)
    return plain_dot(high, table[0]) + (plain_dot(low, table[0]) + plain_dot(high, table[1]))


def sine_cosine(angle):
    turns = jnp.floor(angle * (1.0 / math.pi) + 0.5)
    rest = ((angle - turns * PI_HIGH) - turns * PI_MID) - turns * PI_LOW
    odd = turns - 2.0 * jnp.floor(turns * 0.5)
    sign = 1.0 - 2.0 * odd
    square = rest * rest
    sine = 1.0 / math.factorial(13)
    for degree in (11, 9, 7, 5, 3, 1):
        sine = sine * square + (-1.0) ** (degree // 2) / math.factorial(degree)
    cosine = 1.0 / math.factorial(12)
    for degree in (10, 8, 6, 4, 2, 0):
        cosine = cosine * square + (-1.0) ** (degree // 2) / math.factorial(degree)
    return sine * (rest * sign), cosine * sign


def identity(size):
    rows = lax.broadcasted_iota(jnp.int32, (size, size), 0)
    cols = lax.broadcasted_iota(jnp.int32, (size, size), 1)
    return jnp.where(rows == cols, 1.0, 0.0).astype(F32)


def kernel(
    ctx_count,
    z_count,
    x_count,
    decay,
    skip,
    out_gate,
    in_gate,
    signal,
    grad_out,
    position_table,
    embed_weight,
    hidden_weight,
    filter_weight,
    first_table,
    last_table,
    second_table,
    back_table,
    twist,
    mixed,
    out_gate_grad,
    in_gate_grad,
    signal_grad,
    embed_grad,
    hidden_grad,
    filter_grad,
    skip_grad,
    position_grad,
    pair_send,
    pair_recv,
    raw_send,
    raw_recv,
    grad_send,
    grad_recv,
    inner_send,
    inner_recv,
    weight_all,
    weight_own,
    weight_turned,
    spread_send,
    spread_recv,
    part_send,
    part_recv,
    sum_send,
    sum_recv,
    total_recv,
    slab_send,
    slab_recv,
    place_send,
    place_recv,
    act_one_keep,
    act_two_keep,
    cos_one_keep,
    cos_two_keep,
    pair_sems,
    raw_sems,
    grad_sems,
    inner_sems,
    weight_sems,
    spread_sems,
    part_sems,
    sum_sems,
    total_sems,
    slab_sems,
    place_sems,
):
    chan_count = z_count * x_count
    rows = z_count
    channels = ctx_count
    hidden = hidden_weight.shape[0]
    features = position_table.shape[0]
    part_rows = hidden // z_count
    me = lax.axis_index("ctx")
    my_chan = lax.axis_index("chan")
    my_z = my_chan // x_count
    my_x = my_chan % x_count
    scale = (ctx_count * rows * LANES) ** (-0.5)

    def span(index, size):
        return pl.ds(pl.multiple_of(index * size, size), size)

    def ctx_copy(step, source, target, sems):
        peer = (me + step) % ctx_count
        return pltpu.make_async_remote_copy(
            src_ref=source(peer),
            dst_ref=target(me),
            send_sem=sems.at[0, step],
            recv_sem=sems.at[1, me],
            device_id={"ctx": peer},
            device_id_type=pl.DeviceIdType.MESH,
        )

    def ctx_arrival(step, source, target, sems):
        peer = (me + step) % ctx_count
        return pltpu.make_async_remote_copy(
            src_ref=source(peer),
            dst_ref=target(peer),
            send_sem=sems.at[0, step],
            recv_sem=sems.at[1, peer],
            device_id={"ctx": peer},
            device_id_type=pl.DeviceIdType.MESH,
        )

    def chan_copy(step, source, target, sems):
        peer = (my_chan + step) % chan_count
        return pltpu.make_async_remote_copy(
            src_ref=source(peer),
            dst_ref=target(my_chan),
            send_sem=sems.at[0, step],
            recv_sem=sems.at[1, my_chan],
            device_id={"chan": peer},
            device_id_type=pl.DeviceIdType.MESH,
        )

    def chan_arrival(step, source, target, sems):
        peer = (my_chan + step) % chan_count
        return pltpu.make_async_remote_copy(
            src_ref=source(peer),
            dst_ref=target(peer),
            send_sem=sems.at[0, step],
            recv_sem=sems.at[1, peer],
            device_id={"chan": peer},
            device_id_type=pl.DeviceIdType.MESH,
        )

    def z_copy(step, source, target, sems):
        peer = (my_z + step) % z_count
        return pltpu.make_async_remote_copy(
            src_ref=source(peer),
            dst_ref=target(my_z),
            send_sem=sems.at[0, step],
            recv_sem=sems.at[1, my_z],
            device_id={"chan": peer * x_count + my_x},
            device_id_type=pl.DeviceIdType.MESH,
        )

    def z_arrival(step, source, target, sems):
        peer = (my_z + step) % z_count
        return pltpu.make_async_remote_copy(
            src_ref=source(peer),
            dst_ref=target(peer),
            send_sem=sems.at[0, step],
            recv_sem=sems.at[1, peer],
            device_id={"chan": peer * x_count + my_x},
            device_id_type=pl.DeviceIdType.MESH,
        )

    def each(count, body):
        def one(step, carry):
            body(step)
            return carry

        lax.fori_loop(1, count, one, 0)

    pair_x = (ctx_copy, ctx_arrival, ctx_count,
              lambda p: pair_send.at[:, span(p, rows), :],
              lambda p: pair_recv.at[:, span(p, rows), :], pair_sems)
    raw_x = (ctx_copy, ctx_arrival, ctx_count,
             lambda p: raw_send.at[span(p, rows), :],
             lambda p: raw_recv.at[span(p, rows), :], raw_sems)
    grad_x = (ctx_copy, ctx_arrival, ctx_count,
              lambda p: grad_send.at[span(p, rows), :],
              lambda p: grad_recv.at[span(p, rows), :], grad_sems)
    inner_x = (ctx_copy, ctx_arrival, ctx_count,
               lambda p: inner_send.at[:, span(p, rows), :],
               lambda p: inner_recv.at[:, span(p, rows), :], inner_sems)
    weight_x = (chan_copy, chan_arrival, chan_count,
                lambda p: weight_own,
                lambda p: weight_all.at[span(p, channels), :], weight_sems)
    spread_x = (chan_copy, chan_arrival, chan_count,
                lambda p: spread_send.at[span(p // x_count, channels), :],
                lambda p: spread_recv.at[span(p, channels), :], spread_sems)
    slab_x = (ctx_copy, ctx_arrival, ctx_count,
              lambda p: slab_send, lambda p: slab_recv.at[p], slab_sems)
    part_x = (z_copy, z_arrival, z_count,
              lambda p: part_send.at[span(p, part_rows), :],
              lambda p: part_recv.at[p], part_sems)
    place_x = (z_copy, z_arrival, z_count,
               lambda p: place_send, lambda p: place_recv.at[p], place_sems)
    sum_x = (ctx_copy, ctx_arrival, ctx_count,
             lambda p: sum_send, lambda p: sum_recv.at[p], sum_sems)
    total_x = (z_copy, z_arrival, z_count,
               lambda p: total_recv.at[span(my_z, part_rows), :],
               lambda p: total_recv.at[span(p, part_rows), :], total_sems)

    def send(exchange):
        copy, _, count, source, target, sems = exchange
        each(count, lambda step: copy(step, source, target, sems).start())

    def arrive(exchange):
        _, arrival, count, source, target, sems = exchange
        each(count, lambda step: arrival(step, source, target, sems).wait_recv())

    def sent(exchange):
        copy, _, count, source, target, sems = exchange
        each(count, lambda step: copy(step, source, target, sems).wait_send())

    barrier = pltpu.get_barrier_semaphore()

    def greet_ctx(step):
        pl.semaphore_signal(
            barrier, inc=1, device_id={"ctx": (me + step) % ctx_count},
            device_id_type=pl.DeviceIdType.MESH,
        )

    def greet_chan(step):
        pl.semaphore_signal(
            barrier, inc=1, device_id={"chan": (my_chan + step) % chan_count},
            device_id_type=pl.DeviceIdType.MESH,
        )

    each(chan_count, greet_chan)
    each(ctx_count, greet_ctx)

    product = in_gate[...].astype(F32) * signal[...].astype(F32)
    through = grad_out[...].astype(F32) * out_gate[...].astype(F32)
    skip_part = jnp.sum(product * through, axis=1, keepdims=True)
    for row in range(rows):
        cut = slice(row * LANES, (row + 1) * LANES)
        pair_send[0, pl.ds(row, channels, stride=rows), :] = product[:, cut]
        pair_send[1, pl.ds(row, channels, stride=rows), :] = through[:, cut]
    weight_own[...] = jnp.zeros_like(weight_own)
    weight_own[:, 0:hidden] = exact_dot(identity(channels), filter_weight[...], 1, 1)

    pre_one = exact_dot(embed_weight[...], position_table[...], 0, 0)
    act_one, cos_one = sine_cosine(pre_one)
    act_one_keep[...] = act_one
    cos_one_keep[...] = cos_one
    pre_two = exact_dot(hidden_weight[...], act_one, 0, 0)
    act_two, cos_two = sine_cosine(pre_two)
    act_two_keep[...] = act_two
    cos_two_keep[...] = cos_two
    raw_filter = exact_dot(weight_own[:, 0:hidden], act_two, 1, 0)
    for row in range(rows):
        cut = slice(row * LANES, (row + 1) * LANES)
        raw_send[pl.ds(row, channels, stride=rows), :] = raw_filter[:, cut]

    pl.semaphore_wait(barrier, ctx_count + chan_count - 2)
    send(pair_x)
    send(raw_x)
    send(weight_x)
    pair_recv[:, span(me, rows), :] = pair_send[:, span(me, rows), :]
    raw_recv[span(me, rows), :] = raw_send[span(me, rows), :]
    weight_all[span(my_chan, channels), :] = weight_own[...]

    turn_cos = twist[0]
    turn_sin = twist[1]
    row_total = channels * rows

    def forward(field):
        half = table_left(first_table, field)
        real, imag = half[0:row_total], half[row_total:]
        turned = jnp.concatenate(
            [real * turn_cos + imag * turn_sin, imag * turn_cos - real * turn_sin], axis=1
        )
        whole = table_right(turned, second_table)
        return whole[:, 0:LANES], whole[:, LANES:]

    def times(first, second):
        real = first[0] * second[0] + first[1] * second[1]
        imag = first[0] * second[1] - first[1] * second[0]
        return jnp.concatenate([real, imag], axis=1)

    def inverse(spectrum):
        half = table_right(spectrum, back_table)
        real, imag = half[:, 0:LANES], half[:, LANES:]
        turned = jnp.concatenate(
            [real * turn_cos - imag * turn_sin, real * turn_sin + imag * turn_cos], axis=0
        )
        return table_left(last_table, turned)

    arrive(pair_x)
    own_product = pair_recv[0]
    own_through = pair_recv[1]
    product_spec = forward(own_product)
    through_spec = forward(own_through)
    kernel_grad = inverse(times(product_spec, through_spec))

    cells = (
        lax.broadcasted_iota(jnp.int32, (row_total, LANES), 0) * LANES
        + lax.broadcasted_iota(jnp.int32, (row_total, LANES), 1)
    ).astype(F32)
    envelope = jnp.exp(-decay[me] * cells)
    arrive(raw_x)
    shaped = raw_recv[...] * envelope
    energy = jnp.sum(jnp.sum(shaped * shaped, axis=0, keepdims=True), axis=1, keepdims=True)
    inverse_norm = lax.rsqrt(energy + EPSILON)
    filter_one = shaped * inverse_norm
    along = jnp.sum(jnp.sum(kernel_grad * filter_one, axis=0, keepdims=True), axis=1, keepdims=True)
    grad_send[...] = (kernel_grad - filter_one * along) * inverse_norm * envelope
    send(grad_x)
    grad_recv[span(me, rows), :] = grad_send[span(me, rows), :]

    filter_spec = forward(filter_one)
    conv = inverse(times((filter_spec[0], -filter_spec[1]), product_spec))
    inner_send[0] = conv + skip[me] * own_product
    back_conv = inverse(times(filter_spec, through_spec))
    inner_send[1] = back_conv + skip[me] * own_through
    send(inner_x)
    inner_recv[:, span(me, rows), :] = inner_send[:, span(me, rows), :]
    arrive(weight_x)
    weight_turned[...] = weight_all[...].T

    arrive(grad_x)
    blocks = []
    for row in range(rows):
        block = grad_recv[pl.ds(row, channels, stride=rows), :]
        spread_send[row * channels:(row + 1) * channels, :] = block
        blocks.append(block)
    send(spread_x)
    spread_recv[span(my_chan, channels), :] = spread_send[span(my_z, channels), :]
    slab_send[...] = jnp.broadcast_to(skip_part, (channels, LANES))
    slab_send[:, 0:hidden] = exact_dot(jnp.concatenate(blocks, axis=1), act_two_keep[...], 1, 1)
    send(slab_x)
    slab_recv[me] = slab_send[...]

    arrive(inner_x)
    for row in range(rows):
        cut = slice(row * LANES, (row + 1) * LANES)
        inner = inner_recv[0, pl.ds(row, channels, stride=rows), :]
        mixed[:, cut] = (out_gate[:, cut].astype(F32) * inner).astype(BF16)
        out_gate_grad[:, cut] = (grad_out[:, cut].astype(F32) * inner).astype(BF16)
        pull = inner_recv[1, pl.ds(row, channels, stride=rows), :]
        in_gate_grad[:, cut] = (pull * signal[:, cut].astype(F32)).astype(BF16)
        signal_grad[:, cut] = (pull * in_gate[:, cut].astype(F32)).astype(BF16)

    arrive(spread_x)
    mine = span(my_z, LANES)
    act_two_grad = exact_dot(weight_turned[0:hidden, :], spread_recv[...], 1, 0)
    pre_two_grad = act_two_grad * cos_two_keep[:, mine]
    act_one_grad = exact_dot(hidden_weight[...], pre_two_grad, 1, 0)
    pre_one_grad = act_one_grad * cos_one_keep[:, mine]
    part_send[...] = jnp.zeros_like(part_send)
    part_send[:, 0:hidden] = exact_dot(act_one_keep[:, mine], pre_two_grad, 1, 1)
    part_send[0:features, hidden:2 * hidden] = exact_dot(
        position_table[:, mine], pre_one_grad, 1, 1
    )
    send(part_x)
    part_recv[my_z] = part_send[span(my_z, part_rows), :]
    place_send[...] = jnp.zeros_like(place_send)
    place_send[0:features, :] = exact_dot(embed_weight[...], pre_one_grad, 1, 0)
    send(place_x)
    place_recv[my_z] = place_send[...]

    arrive(part_x)
    sum_send[...] = jnp.sum(part_recv[...], axis=0)
    send(sum_x)
    sum_recv[me] = sum_send[...]

    arrive(slab_x)
    slab = jnp.sum(slab_recv[...], axis=0) * scale
    filter_grad[...] = exact_dot(identity(hidden), slab[:, 0:hidden], 1, 1)
    picks = lax.broadcasted_iota(jnp.int32, (8, LANES), 1) == hidden
    skip_grad[...] = exact_dot(jnp.where(picks, 1.0, 0.0).astype(F32), slab, 1, 1)[0:1]
    arrive(place_x)
    for row in range(rows):
        position_grad[:, row * LANES:(row + 1) * LANES] = place_recv[row, 0:features, :]

    arrive(sum_x)
    total_recv[span(my_z, part_rows), :] = jnp.sum(sum_recv[...], axis=0) * scale
    send(total_x)
    for exchange in (pair_x, raw_x, weight_x, grad_x, inner_x, spread_x, slab_x, part_x, place_x, sum_x):
        sent(exchange)
    arrive(total_x)
    hidden_grad[...] = total_recv[:, 0:hidden]
    embed_grad[...] = total_recv[0:features, hidden:2 * hidden]
    sent(total_x)


def shards(
    x_count,
    out_gate,
    in_gate,
    signal,
    grad_out,
    position_table,
    embed_weight,
    hidden_weight,
    filter_weight,
    decay_rate,
    skip_gain,
):
    channels, length = signal.shape
    ctx_count = lax.axis_size("ctx")
    chan_count = lax.axis_size("chan")
    z_count = chan_count // x_count
    features, hidden = embed_weight.shape
    assert channels == ctx_count and length == z_count * LANES
    row_total = channels * z_count
    part_rows = hidden // z_count
    place_rows = (features + 7) // 8 * 8
    vmem = pl.BlockSpec(memory_space=pltpu.VMEM)
    smem = pl.BlockSpec(memory_space=pltpu.SMEM)
    block = jax.ShapeDtypeStruct((channels, length), BF16)
    scratch = [
        pltpu.VMEM((2, row_total, LANES), F32),
        pltpu.VMEM((2, row_total, LANES), F32),
        pltpu.VMEM((row_total, LANES), F32),
        pltpu.VMEM((row_total, LANES), F32),
        pltpu.VMEM((row_total, LANES), F32),
        pltpu.VMEM((row_total, LANES), F32),
        pltpu.VMEM((2, row_total, LANES), F32),
        pltpu.VMEM((2, row_total, LANES), F32),
        pltpu.VMEM((chan_count * channels, LANES), F32),
        pltpu.VMEM((channels, LANES), F32),
        pltpu.VMEM((LANES, chan_count * channels), F32),
        pltpu.VMEM((row_total, LANES), F32),
        pltpu.VMEM((chan_count * channels, LANES), F32),
        pltpu.VMEM((hidden, LANES), F32),
        pltpu.VMEM((z_count, part_rows, LANES), F32),
        pltpu.VMEM((part_rows, LANES), F32),
        pltpu.VMEM((ctx_count, part_rows, LANES), F32),
        pltpu.VMEM((hidden, LANES), F32),
        pltpu.VMEM((channels, LANES), F32),
        pltpu.VMEM((ctx_count, channels, LANES), F32),
        pltpu.VMEM((place_rows, LANES), F32),
        pltpu.VMEM((z_count, place_rows, LANES), F32),
        pltpu.VMEM((hidden, length), F32),
        pltpu.VMEM((hidden, length), F32),
        pltpu.VMEM((hidden, length), F32),
        pltpu.VMEM((hidden, length), F32),
    ]
    sem_counts = (
        [ctx_count] * 4 + [chan_count] * 2 + [z_count, ctx_count, z_count, ctx_count, z_count]
    )
    scratch += [pltpu.SemaphoreType.DMA((2, count)) for count in sem_counts]
    results = pl.pallas_call(
        functools.partial(kernel, ctx_count, z_count, x_count),
        out_shape=(
            block,
            block,
            block,
            block,
            jax.ShapeDtypeStruct((features, hidden), F32),
            jax.ShapeDtypeStruct((hidden, hidden), F32),
            jax.ShapeDtypeStruct((hidden, channels), F32),
            jax.ShapeDtypeStruct((1, channels), F32),
            jax.ShapeDtypeStruct((features, length), F32),
        ),
        in_specs=[smem] * 2 + [vmem] * 13,
        out_specs=tuple([vmem] * 9),
        scratch_shapes=scratch,
        compiler_params=pltpu.CompilerParams(
            collective_id=0, has_side_effects=True, vmem_limit_bytes=48 * 1024 * 1024
        ),
    )(
        decay_rate,
        skip_gain,
        out_gate,
        in_gate,
        signal,
        grad_out,
        position_table,
        embed_weight,
        hidden_weight,
        filter_weight,
        *(jnp.asarray(table) for table in tables(row_total)),
    )
    return results[:7] + (results[7].reshape(channels),) + results[8:]


def solution(mesh, x_count=X_CHIPS):
    placed = (
        P("chan", "ctx"),
        P("chan", "ctx"),
        P("chan", "ctx"),
        P("chan", "ctx"),
        P(None, "ctx"),
        P(),
        P(),
        P(None, "chan"),
        P("chan"),
        P("chan"),
    )
    return jax.shard_map(
        functools.partial(shards, x_count),
        mesh=mesh,
        in_specs=placed,
        out_specs=(
            P("chan", "ctx"),
            P("chan", "ctx"),
            P("chan", "ctx"),
            P("chan", "ctx"),
            P(),
            P(),
            P(None, "chan"),
            P("chan"),
            P(None, "ctx"),
        ),
        check_vma=False,
    )
```

```python
import functools
import math

import jax
import jax.numpy as jnp
import ml_dtypes
import numpy as np
from jax import lax
from jax.experimental import pallas as pl
from jax.experimental.pallas import tpu as pltpu
from jax.sharding import PartitionSpec as P

EPSILON = 1e-06
F32 = jnp.float32
BF16 = jnp.bfloat16
LANES = 128
X_CHIPS = 4
INPUTS = 13
PI_HIGH = 3.140625
PI_MID = 9.67502593994140625e-4
PI_LOW = 1.509957990978376432e-7


def halves(table):
    high = table.astype(ml_dtypes.bfloat16)
    low = (table - high.astype(np.float64)).astype(ml_dtypes.bfloat16)
    return np.stack([high, low])


@functools.lru_cache(maxsize=None)
def tables(row_count):
    total = 2 * row_count * LANES
    ids = np.arange(row_count)
    lane_ids = np.arange(LANES)
    angle = 2 * np.pi * np.outer(ids + 0.5, ids) / (2 * row_count)
    first = np.concatenate([np.cos(angle), -np.sin(angle)], axis=0)
    last = first.T * (2.0 / total)
    lane_angle = 2 * np.pi * np.outer(lane_ids, lane_ids) / LANES
    cosine, sine = np.cos(lane_angle), np.sin(lane_angle)
    second = np.block([[cosine, -sine], [sine, cosine]])
    twist_angle = 2 * np.pi * np.outer(ids + 0.5, lane_ids) / total
    twist = np.stack([np.cos(twist_angle), np.sin(twist_angle)]).astype(np.float32)
    return halves(first), halves(last), halves(second), halves(second.T), twist


def exact_dot(left, right, left_dim, right_dim):
    return lax.dot_general(
        left,
        right,
        (((left_dim,), (right_dim,)), ((), ())),
        precision=lax.Precision.HIGHEST,
        preferred_element_type=F32,
    )


def split(value):
    high = value.astype(BF16)
    return high, (value - high.astype(F32)).astype(BF16)


def pair_dot(left, right, left_dim, right_dim):
    def one(first, second):
        return lax.dot_general(
            first, second, (((left_dim,), (right_dim,)), ((), ())), preferred_element_type=F32
        )

    return one(left[0], right[0]) + (one(left[0], right[1]) + one(left[1], right[0]))


def sine_cosine(angle):
    turns = jnp.floor(angle * (1.0 / math.pi) + 0.5)
    rest = ((angle - turns * PI_HIGH) - turns * PI_MID) - turns * PI_LOW
    odd = turns - 2.0 * jnp.floor(turns * 0.5)
    sign = 1.0 - 2.0 * odd
    square = rest * rest
    sine = 1.0 / math.factorial(13)
    for degree in (11, 9, 7, 5, 3, 1):
        sine = sine * square + (-1.0) ** (degree // 2) / math.factorial(degree)
    cosine = 1.0 / math.factorial(12)
    for degree in (10, 8, 6, 4, 2, 0):
        cosine = cosine * square + (-1.0) ** (degree // 2) / math.factorial(degree)
    return sine * (rest * sign), cosine * sign


def identity(size):
    rows = lax.broadcasted_iota(jnp.int32, (size, size), 0)
    cols = lax.broadcasted_iota(jnp.int32, (size, size), 1)
    return jnp.where(rows == cols, 1.0, 0.0).astype(F32)


def far_first(count):
    return sorted(range(1, count), key=lambda step: -min(step, count - step))


def kernel(ctx_count, z_count, x_count, decay, skip, *refs):
    sources, refs = refs[:INPUTS], refs[INPUTS:]
    (mixed, out_gate_grad, in_gate_grad, signal_grad, embed_grad, hidden_grad, filter_grad,
     skip_grad, position_grad), refs = refs[:9], refs[9:]
    locals_of, refs = refs[:INPUTS], refs[INPUTS:]
    (in_gate, signal, grad_out, out_gate, embed_weight, position_table, hidden_weight,
     filter_weight, first_ref, last_ref, second_ref, back_ref, twist) = locals_of
    (pair_send, pair_recv, raw_send, raw_recv, grad_send, grad_recv, inner_send, inner_recv,
     slab_send, slab_recv, part_send, part_recv, sum_send, sum_recv, total_recv,
     place_send, place_recv, place_sum, place_all), refs = refs[:19], refs[19:]
    (load_sems, pair_sems, raw_sems, grad_sems, inner_sems, slab_sems, part_sems, sum_sems,
     total_sems, place_sems, extra_sems, spread_sems, extra_spread_sems) = refs

    chan_count = z_count * x_count
    rows = z_count
    channels = ctx_count
    hidden = hidden_weight.shape[0]
    features = position_table.shape[0]
    part_rows = hidden // z_count
    me = lax.axis_index("ctx")
    my_chan = lax.axis_index("chan")
    my_z = my_chan // x_count
    my_x = my_chan % x_count
    scale = (ctx_count * rows * LANES) ** (-0.5)

    loads = {}
    for num, (source, local) in enumerate(zip(sources, locals_of)):
        loads[num] = pltpu.make_async_copy(source, local, load_sems.at[num])
        loads[num].start()

    def span(index, size):
        return pl.ds(pl.multiple_of(index * size, size), size)

    def ctx_peer(step):
        peer = (me + step) % ctx_count
        return peer, {"ctx": peer}

    def chan_peer(step):
        z_step, x_step = step // x_count, step % x_count
        peer = (my_z + z_step) % z_count * x_count + (my_x + x_step) % x_count
        return peer, {"chan": peer}

    def z_peer(step):
        peer = (my_z + step) % z_count
        return peer, {"chan": peer * x_count + my_x}

    def chan_far(step):
        z_step, x_step = step // x_count, step % x_count
        return -(min(z_step, z_count - z_step) + min(x_step, x_count - x_step))

    ctx_steps = far_first(ctx_count)
    z_steps = far_first(z_count)
    chan_steps = sorted(range(1, chan_count), key=chan_far)
    over_ctx = (ctx_peer, me, ctx_steps)
    over_chan = (chan_peer, my_chan, chan_steps)
    over_z = (z_peer, my_z, z_steps)

    def copy_of(exchange, step, slot):
        (peer_of, own, _), source, target, sems = exchange
        peer, device = peer_of(step)
        slot_index = own if slot == "own" else peer
        return pltpu.make_async_remote_copy(
            src_ref=source(peer),
            dst_ref=target(slot_index),
            send_sem=sems.at[0, step],
            recv_sem=sems.at[1, slot_index],
            device_id=device,
            device_id_type=pl.DeviceIdType.MESH,
        )

    def send(exchange):
        for step in exchange[0][2]:
            copy_of(exchange, step, "own").start()

    def arrive(exchange):
        for step in reversed(exchange[0][2]):
            copy_of(exchange, step, "peer").wait_recv()

    def sent(exchange):
        for step in exchange[0][2]:
            copy_of(exchange, step, "own").wait_send()

    pair_x = (over_ctx, lambda p: pair_send.at[:, span(p, rows), :],
              lambda p: pair_recv.at[:, span(p, rows), :], pair_sems)
    raw_x = (over_ctx, lambda p: raw_send.at[span(p, rows), :],
             lambda p: raw_recv.at[span(p, rows), :], raw_sems)
    grad_x = (over_ctx, lambda p: grad_send.at[span(p, rows), :],
              lambda p: grad_recv.at[span(p, rows), :], grad_sems)
    inner_x = (over_ctx, lambda p: inner_send.at[:, span(p, rows), :],
               lambda p: inner_recv.at[:, span(p, rows), :], inner_sems)
    slab_x = (over_ctx, lambda p: slab_send, lambda p: slab_recv.at[p], slab_sems)
    part_x = (over_chan, lambda p: part_send.at[span(p // x_count, part_rows), :],
              lambda p: part_recv.at[p], part_sems)
    sum_x = (over_ctx, lambda p: sum_send, lambda p: sum_recv.at[p], sum_sems)
    total_x = (over_z, lambda p: total_recv.at[span(my_z, part_rows), :],
               lambda p: total_recv.at[span(p, part_rows), :], total_sems)
    place_x = (over_chan, lambda p: place_send.at[span(p, rows), :], lambda p: place_recv.at[0, p], place_sems)
    spread_x = (over_chan, lambda p: place_sum.at[0],
                lambda p: place_all.at[span(p, rows), :], spread_sems)
    extras = range(chan_count, features)

    def extra_x(num):
        return (over_chan, lambda p: place_send.at[pl.ds(num * rows, rows), :],
                lambda p: place_recv.at[1 + num - chan_count, p],
                extra_sems.at[num - chan_count])

    def extra_spread_x(num):
        return (over_chan, lambda p: place_sum.at[1 + num - chan_count],
                lambda p: place_all.at[pl.ds(num * rows, rows), :],
                extra_spread_sems.at[num - chan_count])

    barrier = pltpu.get_barrier_semaphore()
    for step in chan_steps:
        pl.semaphore_signal(barrier, inc=1, device_id=chan_peer(step)[1],
                            device_id_type=pl.DeviceIdType.MESH)
    for step in ctx_steps:
        pl.semaphore_signal(barrier, inc=1, device_id=ctx_peer(step)[1],
                            device_id_type=pl.DeviceIdType.MESH)

    for num in range(4):
        loads[num].wait()
    product = in_gate[...].astype(F32) * signal[...].astype(F32)
    through = grad_out[...].astype(F32) * out_gate[...].astype(F32)
    skip_part = jnp.sum(product * through, axis=1, keepdims=True)
    for row in range(rows):
        cut = slice(row * LANES, (row + 1) * LANES)
        pair_send[0, pl.ds(row, channels, stride=rows), :] = product[:, cut]
        pair_send[1, pl.ds(row, channels, stride=rows), :] = through[:, cut]

    for num in range(4, 8):
        loads[num].wait()
    pre_one = exact_dot(embed_weight[...], position_table[...], 0, 0)
    act_one, cos_one = sine_cosine(pre_one)
    pre_two = exact_dot(hidden_weight[...], act_one, 0, 0)
    act_two, cos_two = sine_cosine(pre_two)
    act_two_halves = split(act_two)
    filter_halves = split(filter_weight[...])
    raw_filter = pair_dot(filter_halves, act_two_halves, 1, 0)
    for row in range(rows):
        cut = slice(row * LANES, (row + 1) * LANES)
        raw_send[pl.ds(row, channels, stride=rows), :] = raw_filter[:, cut]

    pl.semaphore_wait(barrier, ctx_count + chan_count - 2)
    send(pair_x)
    send(raw_x)
    pair_recv[:, span(me, rows), :] = pair_send[:, span(me, rows), :]
    raw_recv[span(me, rows), :] = raw_send[span(me, rows), :]
    for num in range(8, INPUTS):
        loads[num].wait()

    turn_cos = twist[0]
    turn_sin = twist[1]
    row_total = channels * rows

    def both(table):
        return table[0], table[1]

    def forward(fields):
        half = pair_dot(both(first_ref), split(jnp.concatenate(fields, axis=1)), 1, 0)
        turned = []
        for num in range(len(fields)):
            cut = slice(num * LANES, (num + 1) * LANES)
            real, imag = half[0:row_total, cut], half[row_total:, cut]
            turned.append(jnp.concatenate(
                [real * turn_cos + imag * turn_sin, imag * turn_cos - real * turn_sin], axis=1
            ))
        whole = pair_dot(split(jnp.concatenate(turned, axis=0)), both(second_ref), 1, 0)
        return [(whole[num * row_total:(num + 1) * row_total, 0:LANES],
                 whole[num * row_total:(num + 1) * row_total, LANES:]) for num in range(len(fields))]

    def times(first, second):
        real = first[0] * second[0] + first[1] * second[1]
        imag = first[0] * second[1] - first[1] * second[0]
        return jnp.concatenate([real, imag], axis=1)

    def inverse(spectra):
        half = pair_dot(split(jnp.concatenate(spectra, axis=0)), both(back_ref), 1, 0)
        turned = []
        for num in range(len(spectra)):
            cut = slice(num * row_total, (num + 1) * row_total)
            real, imag = half[cut, 0:LANES], half[cut, LANES:]
            turned.append(jnp.concatenate(
                [real * turn_cos - imag * turn_sin, real * turn_sin + imag * turn_cos], axis=0
            ))
        return pair_dot(both(last_ref), split(jnp.concatenate(turned, axis=1)), 1, 0)

    cells = (
        lax.broadcasted_iota(jnp.int32, (row_total, LANES), 0) * LANES
        + lax.broadcasted_iota(jnp.int32, (row_total, LANES), 1)
    ).astype(F32)
    envelope = jnp.exp(-decay[me] * cells)

    arrive(pair_x)
    own_product = pair_recv[0]
    own_through = pair_recv[1]
    product_spec, through_spec = forward([own_product, own_through])
    kernel_grad = inverse([times(product_spec, through_spec)])

    arrive(raw_x)
    shaped = raw_recv[...] * envelope
    energy = jnp.sum(jnp.sum(shaped * shaped, axis=0, keepdims=True), axis=1, keepdims=True)
    inverse_norm = lax.rsqrt(energy + EPSILON)
    filter_one = shaped * inverse_norm
    along = jnp.sum(jnp.sum(kernel_grad * filter_one, axis=0, keepdims=True), axis=1, keepdims=True)
    grad_send[...] = (kernel_grad - filter_one * along) * inverse_norm * envelope
    send(grad_x)
    grad_recv[span(me, rows), :] = grad_send[span(me, rows), :]

    (filter_spec,) = forward([filter_one])
    convs = inverse([
        times((filter_spec[0], -filter_spec[1]), product_spec), times(filter_spec, through_spec)
    ])
    inner_send[0] = convs[:, 0:LANES] + skip[me] * own_product
    inner_send[1] = convs[:, LANES:] + skip[me] * own_through
    send(inner_x)
    inner_recv[:, span(me, rows), :] = inner_send[:, span(me, rows), :]

    arrive(grad_x)
    raw_grad = jnp.concatenate(
        [grad_recv[pl.ds(row, channels, stride=rows), :] for row in range(rows)], axis=1
    )
    raw_grad_halves = split(raw_grad)
    pre_two_grad = pair_dot(filter_halves, raw_grad_halves, 0, 0) * cos_two
    pre_two_halves = split(pre_two_grad)
    pre_one_grad = pair_dot(split(hidden_weight[...]), pre_two_halves, 1, 0) * cos_one
    pre_one_halves = split(pre_one_grad)
    part_send[...] = jnp.zeros_like(part_send)
    part_send[:, 0:hidden] = pair_dot(split(act_one), pre_two_halves, 1, 1)
    part_send[0:features, hidden:2 * hidden] = pair_dot(
        split(position_table[...]), pre_one_halves, 1, 1
    )
    send(part_x)
    part_recv[my_chan] = part_send[span(my_z, part_rows), :]
    place = pair_dot(split(embed_weight[...]), pre_one_halves, 1, 0)
    for row in range(rows):
        place_send[pl.ds(row, features, stride=rows), :] = place[:, row * LANES:(row + 1) * LANES]
    send(place_x)
    place_recv[0, my_chan] = place_send[span(my_chan, rows), :]
    for num in extras:
        for step in chan_steps:
            peer = chan_peer(step)[0]

            @pl.when(peer == 0)
            def _():
                copy_of(extra_x(num), step, "own").start()

        place_recv[1 + num - chan_count, my_chan] = place_send[num * rows:(num + 1) * rows, :]
    slab_send[...] = jnp.broadcast_to(skip_part, (channels, LANES))
    slab_send[:, 0:hidden] = pair_dot(raw_grad_halves, act_two_halves, 1, 1)
    send(slab_x)
    slab_recv[me] = slab_send[...]

    arrive(inner_x)
    for row in range(rows):
        cut = slice(row * LANES, (row + 1) * LANES)
        inner = inner_recv[0, pl.ds(row, channels, stride=rows), :]
        mixed[:, cut] = (out_gate[:, cut].astype(F32) * inner).astype(BF16)
        out_gate_grad[:, cut] = (grad_out[:, cut].astype(F32) * inner).astype(BF16)
        pull = inner_recv[1, pl.ds(row, channels, stride=rows), :]
        in_gate_grad[:, cut] = (pull * signal[:, cut].astype(F32)).astype(BF16)
        signal_grad[:, cut] = (pull * in_gate[:, cut].astype(F32)).astype(BF16)

    arrive(part_x)
    sum_send[...] = jnp.sum(part_recv[...], axis=0)
    send(sum_x)
    sum_recv[me] = sum_send[...]

    arrive(place_x)
    place_sum[0] = jnp.sum(place_recv[0], axis=0)
    send(spread_x)
    place_all[span(my_chan, rows), :] = place_sum[0]
    for num in extras:

        @pl.when(my_chan == 0)
        def _():
            arrive(extra_x(num))
            place_sum[1 + num - chan_count] = jnp.sum(place_recv[1 + num - chan_count], axis=0)
            send(extra_spread_x(num))
            place_all[num * rows:(num + 1) * rows, :] = place_sum[1 + num - chan_count]

    arrive(slab_x)
    slab = jnp.sum(slab_recv[...], axis=0) * scale
    filter_grad[...] = slab[:, 0:hidden]
    picks = lax.broadcasted_iota(jnp.int32, (8, LANES), 1) == hidden
    skip_grad[...] = exact_dot(jnp.where(picks, 1.0, 0.0).astype(F32), slab, 1, 1)[0:1]

    arrive(sum_x)
    total_recv[span(my_z, part_rows), :] = jnp.sum(sum_recv[...], axis=0) * scale
    send(total_x)
    for exchange in (pair_x, raw_x, grad_x, inner_x, slab_x, part_x, sum_x, place_x):
        sent(exchange)

    arrive(spread_x)
    for num in extras:

        @pl.when(my_chan == 0)
        def _():
            sent(extra_spread_x(num))

        @pl.when(my_chan != 0)
        def _():
            for step in chan_steps:

                @pl.when(chan_peer(step)[0] == 0)
                def _():
                    copy_of(extra_x(num), step, "own").wait_send()
                    copy_of(extra_spread_x(num), step, "first").wait_recv()

    for row in range(rows):
        position_grad[:, row * LANES:(row + 1) * LANES] = place_all[
            pl.ds(row, features, stride=rows), :
        ]
    sent(spread_x)
    arrive(total_x)
    hidden_grad[...] = total_recv[:, 0:hidden]
    embed_grad[...] = total_recv[0:features, hidden:2 * hidden]
    sent(total_x)


def put_out(*refs):
    count = len(refs) // 2
    copies = [
        pltpu.make_async_copy(refs[num], refs[count + num], refs[-1].at[num]) for num in range(count)
    ]
    for copy in copies:
        copy.start()
    for copy in copies:
        copy.wait()


def shards(
    x_count,
    out_gate,
    in_gate,
    signal,
    grad_out,
    position_table,
    embed_weight,
    hidden_weight,
    filter_weight,
    decay_rate,
    skip_gain,
):
    channels, length = signal.shape
    ctx_count = lax.axis_size("ctx")
    chan_count = lax.axis_size("chan")
    z_count = chan_count // x_count
    features, hidden = embed_weight.shape
    assert channels == ctx_count and length == z_count * LANES
    row_total = channels * z_count
    part_rows = hidden // z_count
    extra_count = max(1, features - chan_count)
    vmem = pl.BlockSpec(memory_space=pltpu.VMEM)
    smem = pl.BlockSpec(memory_space=pltpu.SMEM)
    hbm = pl.BlockSpec(memory_space=pltpu.HBM)
    operands = (
        in_gate,
        signal,
        grad_out,
        out_gate,
        embed_weight,
        position_table,
        hidden_weight,
        filter_weight.T,
        *(jnp.asarray(table) for table in tables(row_total)),
    )
    block = jax.ShapeDtypeStruct((channels, length), BF16)
    shapes = (
        block,
        block,
        block,
        block,
        jax.ShapeDtypeStruct((features, hidden), F32),
        jax.ShapeDtypeStruct((hidden, hidden), F32),
        jax.ShapeDtypeStruct((channels, hidden), F32),
        jax.ShapeDtypeStruct((1, channels), F32),
        jax.ShapeDtypeStruct((features, length), F32),
    )
    scratch = [pltpu.VMEM(operand.shape, operand.dtype) for operand in operands]
    scratch += [
        pltpu.VMEM(shape, F32)
        for shape in (
            (2, row_total, LANES),
            (2, row_total, LANES),
            (row_total, LANES),
            (row_total, LANES),
            (row_total, LANES),
            (row_total, LANES),
            (2, row_total, LANES),
            (2, row_total, LANES),
            (channels, LANES),
            (ctx_count, channels, LANES),
            (hidden, LANES),
            (chan_count, part_rows, LANES),
            (part_rows, LANES),
            (ctx_count, part_rows, LANES),
            (hidden, LANES),
            (features * z_count, LANES),
            (1 + extra_count, chan_count, z_count, LANES),
            (1 + extra_count, z_count, LANES),
            (features * z_count, LANES),
        )
    ]
    scratch += [pltpu.SemaphoreType.DMA((INPUTS,))]
    scratch += [
        pltpu.SemaphoreType.DMA((2, count))
        for count in [ctx_count] * 5 + [chan_count, ctx_count, z_count, chan_count]
    ]
    scratch += [
        pltpu.SemaphoreType.DMA((extra_count, 2, chan_count)),
        pltpu.SemaphoreType.DMA((2, chan_count)),
        pltpu.SemaphoreType.DMA((extra_count, 2, chan_count)),
    ]
    results = pl.pallas_call(
        functools.partial(kernel, ctx_count, z_count, x_count),
        out_shape=shapes,
        in_specs=[smem] * 2 + [hbm] * INPUTS,
        out_specs=tuple([vmem] * 9),
        scratch_shapes=scratch,
        compiler_params=pltpu.CompilerParams(
            collective_id=0, has_side_effects=True, vmem_limit_bytes=67043328
        ),
    )(decay_rate, skip_gain, *operands)
    results = pl.pallas_call(
        put_out,
        out_shape=shapes,
        in_specs=[vmem] * 9,
        out_specs=tuple([hbm] * 9),
        scratch_shapes=[pltpu.SemaphoreType.DMA((9,))],
    )(*results)
    results = list(results)
    results[6] = results[6].T
    results[7] = results[7].reshape(channels)
    return tuple(results)


def solution(mesh, x_count=X_CHIPS):
    placed = (
        P("chan", "ctx"),
        P("chan", "ctx"),
        P("chan", "ctx"),
        P("chan", "ctx"),
        P(None, "ctx"),
        P(),
        P(),
        P(None, "chan"),
        P("chan"),
        P("chan"),
    )
    return jax.shard_map(
        functools.partial(shards, x_count),
        mesh=mesh,
        in_specs=placed,
        out_specs=(
            P("chan", "ctx"),
            P("chan", "ctx"),
            P("chan", "ctx"),
            P("chan", "ctx"),
            P(),
            P(),
            P(None, "chan"),
            P("chan"),
            P(None, "ctx"),
        ),
        check_vma=False,
    )
```

```python
import functools
import math

import jax
import jax.numpy as jnp
import ml_dtypes
import numpy as np
from jax import lax
from jax.experimental import pallas as pl
from jax.experimental.pallas import tpu as pltpu
from jax.sharding import PartitionSpec as P

EPSILON = 1e-06
F32 = jnp.float32
BF16 = jnp.bfloat16
LANES = 128
X_CHIPS = 4
INPUTS = 15
PI_HIGH = 3.140625
PI_MID = 9.67502593994140625e-4
PI_LOW = 1.509957990978376432e-7


def halves(table):
    high = table.astype(ml_dtypes.bfloat16)
    low = (table - high.astype(np.float64)).astype(ml_dtypes.bfloat16)
    return np.stack([high, low])


@functools.lru_cache(maxsize=None)
def tables(row_count):
    total = 2 * row_count * LANES
    ids = np.arange(row_count)
    lane_ids = np.arange(LANES)
    angle = 2 * np.pi * np.outer(ids + 0.5, ids) / (2 * row_count)
    first = np.concatenate([np.cos(angle), -np.sin(angle)], axis=0)
    last = first.T * (2.0 / total)
    lane_angle = 2 * np.pi * np.outer(lane_ids, lane_ids) / LANES
    cosine, sine = np.cos(lane_angle), np.sin(lane_angle)
    second = np.block([[cosine, -sine], [sine, cosine]])
    twist_angle = 2 * np.pi * np.outer(ids + 0.5, lane_ids) / total
    twist = np.stack([np.cos(twist_angle), np.sin(twist_angle)]).astype(np.float32)
    return halves(first), halves(last), halves(second), halves(second.T), twist


def exact_dot(left, right, left_dim, right_dim):
    return lax.dot_general(
        left,
        right,
        (((left_dim,), (right_dim,)), ((), ())),
        precision=lax.Precision.HIGHEST,
        preferred_element_type=F32,
    )


def split(value):
    high = value.astype(BF16)
    return high, (value - high.astype(F32)).astype(BF16)


def pair_dot(left, right, left_dim, right_dim):
    def one(first, second):
        return lax.dot_general(
            first, second, (((left_dim,), (right_dim,)), ((), ())), preferred_element_type=F32
        )

    return one(left[0], right[0]) + (one(left[0], right[1]) + one(left[1], right[0]))


def sine_cosine(angle):
    turns = jnp.floor(angle * (1.0 / math.pi) + 0.5)
    rest = ((angle - turns * PI_HIGH) - turns * PI_MID) - turns * PI_LOW
    odd = turns - 2.0 * jnp.floor(turns * 0.5)
    sign = 1.0 - 2.0 * odd
    square = rest * rest
    sine = 1.0 / math.factorial(13)
    for degree in (11, 9, 7, 5, 3, 1):
        sine = sine * square + (-1.0) ** (degree // 2) / math.factorial(degree)
    cosine = 1.0 / math.factorial(12)
    for degree in (10, 8, 6, 4, 2, 0):
        cosine = cosine * square + (-1.0) ** (degree // 2) / math.factorial(degree)
    return sine * (rest * sign), cosine * sign


def identity(size):
    rows = lax.broadcasted_iota(jnp.int32, (size, size), 0)
    cols = lax.broadcasted_iota(jnp.int32, (size, size), 1)
    return jnp.where(rows == cols, 1.0, 0.0).astype(F32)


def far_first(count):
    return sorted(range(1, count), key=lambda step: -min(step, count - step))


def kernel(ctx_count, z_count, x_count, *refs):
    sources, refs = refs[:INPUTS], refs[INPUTS:]
    (mixed, out_gate_grad, in_gate_grad, signal_grad, embed_grad, hidden_grad, filter_grad,
     skip_grad, position_grad), refs = refs[:9], refs[9:]
    locals_of, refs = refs[:INPUTS], refs[INPUTS:]
    (in_gate, signal, grad_out, out_gate, embed_weight, position_table, hidden_weight,
     filter_weight, decay, skip, first_ref, last_ref, second_ref, back_ref, twist) = locals_of
    (pair_send, pair_recv, raw_send, raw_recv, grad_send, grad_recv, inner_send, inner_recv,
     slab_send, slab_recv, part_send, part_recv, sum_send, sum_recv, total_recv,
     place_send, place_recv, place_sum, place_all), refs = refs[:19], refs[19:]
    (load_sems, pair_sems, raw_sems, grad_sems, inner_sems, slab_sems, part_sems, sum_sems,
     total_sems, place_sems, spread_sems) = refs

    chan_count = z_count * x_count
    rows = z_count
    channels = ctx_count
    hidden = hidden_weight.shape[0]
    features = position_table.shape[0]
    part_rows = hidden // z_count
    me = lax.axis_index("ctx")
    my_chan = lax.axis_index("chan")
    my_z = my_chan // x_count
    my_x = my_chan % x_count
    scale = (ctx_count * rows * LANES) ** (-0.5)

    loads = {}
    for num, (source, local) in enumerate(zip(sources, locals_of)):
        loads[num] = pltpu.make_async_copy(source, local, load_sems.at[num])
        loads[num].start()

    def span(index, size):
        return pl.ds(pl.multiple_of(index * size, size), size)

    def ahead(index, step, count):
        index = index + step
        return jnp.where(index >= count, index - count, index) if step else index

    def ctx_peer(step):
        peer = ahead(me, step, ctx_count)
        return peer, {"ctx": peer}

    def chan_peer(step):
        z_step, x_step = step // x_count, step % x_count
        peer = ahead(my_z, z_step, z_count) * x_count + ahead(my_x, x_step, x_count)
        return peer, {"chan": peer}

    def z_peer(step):
        peer = ahead(my_z, step, z_count)
        return peer, {"chan": peer * x_count + my_x}

    def chan_far(step):
        z_step, x_step = step // x_count, step % x_count
        return -(min(z_step, z_count - z_step) + min(x_step, x_count - x_step))

    ctx_steps = far_first(ctx_count)
    z_steps = far_first(z_count)
    chan_steps = sorted(range(1, chan_count), key=chan_far)
    over_ctx = (ctx_peer, me, ctx_steps)
    over_chan = (chan_peer, my_chan, chan_steps)
    over_z = (z_peer, my_z, z_steps)

    def copy_of(exchange, step, slot):
        (peer_of, own, _), source, target, sems = exchange
        peer, device = peer_of(step)
        slot_index = own if slot == "own" else peer
        return pltpu.make_async_remote_copy(
            src_ref=source(peer),
            dst_ref=target(slot_index),
            send_sem=sems.at[0, step],
            recv_sem=sems.at[1, slot_index],
            device_id=device,
            device_id_type=pl.DeviceIdType.MESH,
        )

    def send(exchange):
        for step in exchange[0][2]:
            copy_of(exchange, step, "own").start()

    def arrive(exchange):
        for step in reversed(exchange[0][2]):
            copy_of(exchange, step, "peer").wait_recv()

    def sent(exchange):
        for step in exchange[0][2]:
            copy_of(exchange, step, "own").wait_send()

    pair_x = (over_ctx, lambda p: pair_send.at[:, span(p, rows), :],
              lambda p: pair_recv.at[:, span(p, rows), :], pair_sems)
    raw_x = (over_ctx, lambda p: raw_send.at[span(p, rows), :],
             lambda p: raw_recv.at[span(p, rows), :], raw_sems)
    grad_x = (over_ctx, lambda p: grad_send.at[span(p, rows), :],
              lambda p: grad_recv.at[span(p, rows), :], grad_sems)
    inner_x = (over_ctx, lambda p: inner_send.at[:, span(p, rows), :],
               lambda p: inner_recv.at[:, span(p, rows), :], inner_sems)
    slab_x = (over_ctx, lambda p: slab_send, lambda p: slab_recv.at[p], slab_sems)
    part_x = (over_chan, lambda p: part_send.at[span(p // x_count, part_rows), :],
              lambda p: part_recv.at[p], part_sems)
    sum_x = (over_ctx, lambda p: sum_send, lambda p: sum_recv.at[p], sum_sems)
    total_x = (over_z, lambda p: total_recv.at[span(my_z, part_rows), :],
               lambda p: total_recv.at[span(p, part_rows), :], total_sems)
    place_x = (over_chan, lambda p: place_send.at[span(p, rows), :], lambda p: place_recv.at[p], place_sems)
    spread_x = (over_chan, lambda p: place_sum,
                lambda p: place_all.at[span(p, rows), :], spread_sems)
    corner = (features + 7) // 8 * 8
    corner_rows = rows * LANES // hidden

    barrier = pltpu.get_barrier_semaphore()
    for step in chan_steps:
        pl.semaphore_signal(barrier, inc=1, device_id=chan_peer(step)[1],
                            device_id_type=pl.DeviceIdType.MESH)
    for step in ctx_steps:
        pl.semaphore_signal(barrier, inc=1, device_id=ctx_peer(step)[1],
                            device_id_type=pl.DeviceIdType.MESH)

    for num in range(4):
        loads[num].wait()
    product = in_gate[...].astype(F32) * signal[...].astype(F32)
    through = grad_out[...].astype(F32) * out_gate[...].astype(F32)
    skip_part = jnp.sum(product * through, axis=1, keepdims=True)
    for row in range(rows):
        cut = slice(row * LANES, (row + 1) * LANES)
        pair_send[0, pl.ds(row, channels, stride=rows), :] = product[:, cut]
        pair_send[1, pl.ds(row, channels, stride=rows), :] = through[:, cut]

    for num in range(4, 10):
        loads[num].wait()
    pre_one = exact_dot(embed_weight[...], position_table[...], 0, 0)
    act_one, cos_one = sine_cosine(pre_one)
    pre_two = exact_dot(hidden_weight[...], act_one, 0, 0)
    act_two, cos_two = sine_cosine(pre_two)
    act_two_halves = split(act_two)
    filter_halves = split(filter_weight[...])
    raw_filter = pair_dot(filter_halves, act_two_halves, 1, 0)
    for row in range(rows):
        cut = slice(row * LANES, (row + 1) * LANES)
        raw_send[pl.ds(row, channels, stride=rows), :] = raw_filter[:, cut]

    pl.semaphore_wait(barrier, ctx_count + chan_count - 2)
    send(pair_x)
    send(raw_x)
    pair_recv[:, span(me, rows), :] = pair_send[:, span(me, rows), :]
    raw_recv[span(me, rows), :] = raw_send[span(me, rows), :]
    for num in range(10, INPUTS):
        loads[num].wait()

    turn_cos = twist[0]
    turn_sin = twist[1]
    row_total = channels * rows

    def both(table):
        return table[0], table[1]

    def forward(fields):
        half = pair_dot(both(first_ref), split(jnp.concatenate(fields, axis=1)), 1, 0)
        turned = []
        for num in range(len(fields)):
            cut = slice(num * LANES, (num + 1) * LANES)
            real, imag = half[0:row_total, cut], half[row_total:, cut]
            turned.append(jnp.concatenate(
                [real * turn_cos + imag * turn_sin, imag * turn_cos - real * turn_sin], axis=1
            ))
        whole = pair_dot(split(jnp.concatenate(turned, axis=0)), both(second_ref), 1, 0)
        return [(whole[num * row_total:(num + 1) * row_total, 0:LANES],
                 whole[num * row_total:(num + 1) * row_total, LANES:]) for num in range(len(fields))]

    def times(first, second):
        real = first[0] * second[0] + first[1] * second[1]
        imag = first[0] * second[1] - first[1] * second[0]
        return jnp.concatenate([real, imag], axis=1)

    def inverse(spectra):
        half = pair_dot(split(jnp.concatenate(spectra, axis=0)), both(back_ref), 1, 0)
        turned = []
        for num in range(len(spectra)):
            cut = slice(num * row_total, (num + 1) * row_total)
            real, imag = half[cut, 0:LANES], half[cut, LANES:]
            turned.append(jnp.concatenate(
                [real * turn_cos - imag * turn_sin, real * turn_sin + imag * turn_cos], axis=0
            ))
        return pair_dot(both(last_ref), split(jnp.concatenate(turned, axis=1)), 1, 0)

    cells = (
        lax.broadcasted_iota(jnp.int32, (row_total, LANES), 0) * LANES
        + lax.broadcasted_iota(jnp.int32, (row_total, LANES), 1)
    ).astype(F32)
    envelope = jnp.exp(-decay[me] * cells)

    arrive(pair_x)
    own_product = pair_recv[0]
    own_through = pair_recv[1]
    product_spec, through_spec = forward([own_product, own_through])
    kernel_grad = inverse([times(product_spec, through_spec)])

    arrive(raw_x)
    shaped = raw_recv[...] * envelope
    energy = jnp.sum(jnp.sum(shaped * shaped, axis=0, keepdims=True), axis=1, keepdims=True)
    inverse_norm = lax.rsqrt(energy + EPSILON)
    filter_one = shaped * inverse_norm
    along = jnp.sum(jnp.sum(kernel_grad * filter_one, axis=0, keepdims=True), axis=1, keepdims=True)
    grad_send[...] = (kernel_grad - filter_one * along) * inverse_norm * envelope
    send(grad_x)
    grad_recv[span(me, rows), :] = grad_send[span(me, rows), :]

    (filter_spec,) = forward([filter_one])
    convs = inverse([
        times((filter_spec[0], -filter_spec[1]), product_spec), times(filter_spec, through_spec)
    ])
    inner_send[0] = convs[:, 0:LANES] + skip[me] * own_product
    inner_send[1] = convs[:, LANES:] + skip[me] * own_through
    send(inner_x)
    inner_recv[:, span(me, rows), :] = inner_send[:, span(me, rows), :]

    arrive(grad_x)
    raw_grad = jnp.concatenate(
        [grad_recv[pl.ds(row, channels, stride=rows), :] for row in range(rows)], axis=1
    )
    raw_grad_halves = split(raw_grad)
    pre_two_grad = pair_dot(filter_halves, raw_grad_halves, 0, 0) * cos_two
    pre_two_halves = split(pre_two_grad)
    pre_one_grad = pair_dot(split(hidden_weight[...]), pre_two_halves, 1, 0) * cos_one
    pre_one_halves = split(pre_one_grad)
    part_send[...] = jnp.zeros_like(part_send)
    part_send[:, 0:hidden] = pair_dot(split(act_one), pre_two_halves, 1, 1)
    part_send[0:features, hidden:2 * hidden] = pair_dot(
        split(position_table[...]), pre_one_halves, 1, 1
    )
    place = pair_dot(split(embed_weight[...]), pre_one_halves, 1, 0)
    for num in range(corner_rows):
        part_send[corner + num:corner + num + 1, hidden:2 * hidden] = place[
            chan_count:features, num * hidden:(num + 1) * hidden
        ]
    send(part_x)
    part_recv[my_chan] = part_send[span(my_z, part_rows), :]
    slab_send[...] = jnp.broadcast_to(skip_part, (channels, LANES))
    slab_send[:, 0:hidden] = pair_dot(raw_grad_halves, act_two_halves, 1, 1)
    send(slab_x)
    slab_recv[me] = slab_send[...]
    for row in range(rows):
        place_send[pl.ds(row, chan_count, stride=rows), :] = place[
            0:chan_count, row * LANES:(row + 1) * LANES
        ]
    send(place_x)
    place_recv[my_chan] = place_send[span(my_chan, rows), :]

    arrive(inner_x)
    for row in range(rows):
        cut = slice(row * LANES, (row + 1) * LANES)
        inner = inner_recv[0, pl.ds(row, channels, stride=rows), :]
        mixed[:, cut] = (out_gate[:, cut].astype(F32) * inner).astype(BF16)
        out_gate_grad[:, cut] = (grad_out[:, cut].astype(F32) * inner).astype(BF16)
        pull = inner_recv[1, pl.ds(row, channels, stride=rows), :]
        in_gate_grad[:, cut] = (pull * signal[:, cut].astype(F32)).astype(BF16)
        signal_grad[:, cut] = (pull * in_gate[:, cut].astype(F32)).astype(BF16)

    arrive(part_x)
    sum_send[...] = jnp.sum(part_recv[...], axis=0)
    send(sum_x)
    sum_recv[me] = sum_send[...]

    arrive(place_x)
    place_sum[...] = jnp.sum(place_recv[...], axis=0)
    send(spread_x)
    place_all[span(my_chan, rows), :] = place_sum[...]

    arrive(slab_x)
    slab = jnp.sum(slab_recv[...], axis=0) * scale
    filter_grad[...] = slab[:, 0:hidden]
    picks = lax.broadcasted_iota(jnp.int32, (8, LANES), 1) == hidden
    skip_grad[...] = exact_dot(jnp.where(picks, 1.0, 0.0).astype(F32), slab, 1, 1)[0:1]

    arrive(sum_x)
    part_row = lax.broadcasted_iota(jnp.int32, (part_rows, LANES), 0) + my_z * part_rows
    part_lane = lax.broadcasted_iota(jnp.int32, (part_rows, LANES), 1)
    in_corner = (part_row >= corner) & (part_row < corner + corner_rows) & (part_lane >= hidden)
    total_recv[span(my_z, part_rows), :] = jnp.where(
        in_corner, sum_send[...], jnp.sum(sum_recv[...], axis=0) * scale
    )
    send(total_x)
    for exchange in (pair_x, raw_x, grad_x, inner_x, slab_x, part_x, sum_x, place_x):
        sent(exchange)

    arrive(spread_x)
    for row in range(rows):
        position_grad[0:chan_count, row * LANES:(row + 1) * LANES] = place_all[
            pl.ds(row, chan_count, stride=rows), :
        ]
    sent(spread_x)
    arrive(total_x)
    hidden_grad[...] = total_recv[:, 0:hidden]
    embed_grad[...] = total_recv[0:features, hidden:2 * hidden]
    for num in range(corner_rows):
        position_grad[chan_count:features, num * hidden:(num + 1) * hidden] = total_recv[
            corner + num:corner + num + 1, hidden:2 * hidden
        ]
    sent(total_x)


def put_out(*refs):
    count = len(refs) // 2
    copies = [
        pltpu.make_async_copy(refs[num], refs[count + num], refs[-1].at[num]) for num in range(count)
    ]
    for copy in copies:
        copy.start()
    for copy in copies:
        copy.wait()


def shards(
    x_count,
    out_gate,
    in_gate,
    signal,
    grad_out,
    position_table,
    embed_weight,
    hidden_weight,
    filter_weight,
    decay_rate,
    skip_gain,
):
    channels, length = signal.shape
    ctx_count = lax.axis_size("ctx")
    chan_count = lax.axis_size("chan")
    z_count = chan_count // x_count
    features, hidden = embed_weight.shape
    assert channels == ctx_count and length == z_count * LANES
    row_total = channels * z_count
    part_rows = hidden // z_count
    assert features == chan_count + 1 and 2 * hidden == LANES
    assert (features + 7) // 8 * 8 + length // hidden <= hidden
    vmem = pl.BlockSpec(memory_space=pltpu.VMEM)
    hbm = pl.BlockSpec(memory_space=pltpu.HBM)
    operands = (
        in_gate,
        signal,
        grad_out,
        out_gate,
        embed_weight,
        position_table,
        hidden_weight,
        filter_weight.T,
        decay_rate,
        skip_gain,
        *(jnp.asarray(table) for table in tables(row_total)),
    )
    block = jax.ShapeDtypeStruct((channels, length), BF16)
    shapes = (
        block,
        block,
        block,
        block,
        jax.ShapeDtypeStruct((features, hidden), F32),
        jax.ShapeDtypeStruct((hidden, hidden), F32),
        jax.ShapeDtypeStruct((channels, hidden), F32),
        jax.ShapeDtypeStruct((1, channels), F32),
        jax.ShapeDtypeStruct((features, length), F32),
    )
    scratch = [
        (pltpu.VMEM if operand.ndim > 1 else pltpu.SMEM)(operand.shape, operand.dtype)
        for operand in operands
    ]
    scratch += [
        pltpu.VMEM(shape, F32)
        for shape in (
            (2, row_total, LANES),
            (2, row_total, LANES),
            (row_total, LANES),
            (row_total, LANES),
            (row_total, LANES),
            (row_total, LANES),
            (2, row_total, LANES),
            (2, row_total, LANES),
            (channels, LANES),
            (ctx_count, channels, LANES),
            (hidden, LANES),
            (chan_count, part_rows, LANES),
            (part_rows, LANES),
            (ctx_count, part_rows, LANES),
            (hidden, LANES),
            (chan_count * z_count, LANES),
            (chan_count, z_count, LANES),
            (z_count, LANES),
            (chan_count * z_count, LANES),
        )
    ]
    scratch += [pltpu.SemaphoreType.DMA((INPUTS,))]
    scratch += [
        pltpu.SemaphoreType.DMA((2, count))
        for count in [ctx_count] * 5 + [chan_count, ctx_count, z_count, chan_count, chan_count]
    ]
    results = pl.pallas_call(
        functools.partial(kernel, ctx_count, z_count, x_count),
        out_shape=shapes,
        in_specs=[hbm] * INPUTS,
        out_specs=tuple([vmem] * 9),
        scratch_shapes=scratch,
        compiler_params=pltpu.CompilerParams(
            collective_id=0, has_side_effects=True, vmem_limit_bytes=40 * 1024 * 1024
        ),
    )(*(pltpu.with_memory_space_constraint(operand, pltpu.HBM) for operand in operands))
    results = pl.pallas_call(
        put_out,
        out_shape=tuple(pltpu.HBM(shape.shape, shape.dtype) for shape in shapes),
        in_specs=[vmem] * 9,
        out_specs=tuple([hbm] * 9),
        scratch_shapes=[pltpu.SemaphoreType.DMA((9,))],
        compiler_params=pltpu.CompilerParams(vmem_limit_bytes=4 * 1024 * 1024),
    )(*results)
    results = list(results)
    results[6] = results[6].T
    results[7] = results[7].reshape(channels)
    return tuple(results)


def solution(mesh, x_count=X_CHIPS):
    placed = (
        P("chan", "ctx"),
        P("chan", "ctx"),
        P("chan", "ctx"),
        P("chan", "ctx"),
        P(None, "ctx"),
        P(),
        P(),
        P(None, "chan"),
        P("chan"),
        P("chan"),
    )
    return jax.shard_map(
        functools.partial(shards, x_count),
        mesh=mesh,
        in_specs=placed,
        out_specs=(
            P("chan", "ctx"),
            P("chan", "ctx"),
            P("chan", "ctx"),
            P("chan", "ctx"),
            P(),
            P(),
            P(None, "chan"),
            P("chan"),
            P(None, "ctx"),
        ),
        check_vma=False,
    )
```

```python
import functools
import math

import jax
import jax.numpy as jnp
import ml_dtypes
import numpy as np
from jax import lax
from jax.experimental import pallas as pl
from jax.experimental.pallas import tpu as pltpu
from jax.sharding import PartitionSpec as P

EPSILON = 1e-06
F32 = jnp.float32
BF16 = jnp.bfloat16
LANES = 128
X_CHIPS = 4
INPUTS = 15
PI_HIGH = 3.140625
PI_MID = 9.67502593994140625e-4
PI_LOW = 1.509957990978376432e-7


def halves(table):
    high = table.astype(ml_dtypes.bfloat16)
    low = (table - high.astype(np.float64)).astype(ml_dtypes.bfloat16)
    return np.stack([high, low])


@functools.lru_cache(maxsize=None)
def tables(row_count):
    total = 2 * row_count * LANES
    ids = np.arange(row_count)
    lane_ids = np.arange(LANES)
    angle = 2 * np.pi * np.outer(ids + 0.5, ids) / (2 * row_count)
    first = np.concatenate([np.cos(angle), -np.sin(angle)], axis=0)
    last = first.T * (2.0 / total)
    lane_angle = 2 * np.pi * np.outer(lane_ids, lane_ids) / LANES
    cosine, sine = np.cos(lane_angle), np.sin(lane_angle)
    second = np.block([[cosine, -sine], [sine, cosine]])
    twist_angle = 2 * np.pi * np.outer(ids + 0.5, lane_ids) / total
    twist = np.stack([np.cos(twist_angle), np.sin(twist_angle)]).astype(np.float32)
    return halves(first), halves(last), halves(second), halves(second.T), twist


def exact_dot(left, right, left_dim, right_dim):
    return lax.dot_general(
        left,
        right,
        (((left_dim,), (right_dim,)), ((), ())),
        precision=lax.Precision.HIGHEST,
        preferred_element_type=F32,
    )


def split(value):
    high = value.astype(BF16)
    return high, (value - high.astype(F32)).astype(BF16)


def pair_dot(left, right, left_dim, right_dim):
    def one(first, second):
        return lax.dot_general(
            first, second, (((left_dim,), (right_dim,)), ((), ())), preferred_element_type=F32
        )

    return one(left[0], right[0]) + (one(left[0], right[1]) + one(left[1], right[0]))


def sine_cosine(angle):
    turns = jnp.floor(angle * (1.0 / math.pi) + 0.5)
    rest = ((angle - turns * PI_HIGH) - turns * PI_MID) - turns * PI_LOW
    odd = turns - 2.0 * jnp.floor(turns * 0.5)
    sign = 1.0 - 2.0 * odd
    square = rest * rest
    sine = 1.0 / math.factorial(13)
    for degree in (11, 9, 7, 5, 3, 1):
        sine = sine * square + (-1.0) ** (degree // 2) / math.factorial(degree)
    cosine = 1.0 / math.factorial(12)
    for degree in (10, 8, 6, 4, 2, 0):
        cosine = cosine * square + (-1.0) ** (degree // 2) / math.factorial(degree)
    return sine * (rest * sign), cosine * sign


def identity(size):
    rows = lax.broadcasted_iota(jnp.int32, (size, size), 0)
    cols = lax.broadcasted_iota(jnp.int32, (size, size), 1)
    return jnp.where(rows == cols, 1.0, 0.0).astype(F32)


def far_first(count):
    return sorted(range(1, count), key=lambda step: -min(step, count - step))


def kernel(ctx_count, z_count, x_count, *refs):
    sources, refs = refs[:INPUTS], refs[INPUTS:]
    (mixed, out_gate_grad, in_gate_grad, signal_grad, embed_grad, hidden_grad, filter_grad,
     skip_grad, position_grad), refs = refs[:9], refs[9:]
    locals_of, refs = refs[:INPUTS], refs[INPUTS:]
    (in_gate, signal, grad_out, out_gate, embed_weight, position_table, hidden_weight,
     filter_weight, decay, skip, first_ref, last_ref, second_ref, back_ref, twist) = locals_of
    (pair_send, pair_recv, raw_send, raw_recv, grad_send, grad_recv, inner_send, inner_recv,
     slab_send, slab_recv, part_send, part_recv, sum_send, sum_recv, total_recv,
     place_send, place_recv, place_sum, place_all, act_one_keep, act_two_keep, position_keep,
     hidden_keep, embed_keep, cos_one_keep, cos_two_keep), refs = refs[:26], refs[26:]
    (load_sems, pair_sems, raw_sems, grad_sems, inner_sems, slab_sems, part_sems, sum_sems,
     total_sems, place_sems, spread_sems, round_sems) = refs

    chan_count = z_count * x_count
    rows = z_count
    channels = ctx_count
    hidden = hidden_weight.shape[0]
    features = position_table.shape[0]
    part_rows = hidden // z_count
    me = lax.axis_index("ctx")
    my_chan = lax.axis_index("chan")
    my_z = my_chan // x_count
    my_x = my_chan % x_count
    scale = (ctx_count * rows * LANES) ** (-0.5)

    loads = {}
    for num, (source, local) in enumerate(zip(sources, locals_of)):
        loads[num] = pltpu.make_async_copy(source, local, load_sems.at[num])
        loads[num].start()

    def span(index, size):
        return pl.ds(pl.multiple_of(index * size, size), size)

    def ahead(index, step, count):
        index = index + step
        return jnp.where(index >= count, index - count, index) if step else index

    def ctx_peer(step):
        peer = ahead(me, step, ctx_count)
        return peer, {"ctx": peer}

    def chan_peer(step):
        z_step, x_step = step // x_count, step % x_count
        peer = ahead(my_z, z_step, z_count) * x_count + ahead(my_x, x_step, x_count)
        return peer, {"chan": peer}

    def z_peer(step):
        peer = ahead(my_z, step, z_count)
        return peer, {"chan": peer * x_count + my_x}

    def chan_far(step):
        z_step, x_step = step // x_count, step % x_count
        return -(min(z_step, z_count - z_step) + min(x_step, x_count - x_step))

    ctx_steps = far_first(ctx_count)
    z_steps = far_first(z_count)
    chan_steps = sorted(range(1, chan_count), key=chan_far)
    over_ctx = (ctx_peer, me, ctx_steps)
    over_chan = (chan_peer, my_chan, chan_steps)
    over_z = (z_peer, my_z, z_steps)

    def copy_of(exchange, step, slot):
        (peer_of, own, _), source, target, sems = exchange
        peer, device = peer_of(step)
        slot_index = own if slot == "own" else peer
        return pltpu.make_async_remote_copy(
            src_ref=source(peer),
            dst_ref=target(slot_index),
            send_sem=sems.at[0, step],
            recv_sem=sems.at[1, slot_index],
            device_id=device,
            device_id_type=pl.DeviceIdType.MESH,
        )

    def send(exchange):
        for step in exchange[0][2]:
            copy_of(exchange, step, "own").start()

    def arrive(exchange):
        for step in reversed(exchange[0][2]):
            copy_of(exchange, step, "peer").wait_recv()

    def sent(exchange):
        for step in exchange[0][2]:
            copy_of(exchange, step, "own").wait_send()

    def both(table):
        return table[0], table[1]

    def keep_halves(keep, value):
        keep[0], keep[1] = split(value)

    pair_x = (over_ctx, lambda p: pair_send.at[:, span(p, rows), :],
              lambda p: pair_recv.at[:, span(p, rows), :], pair_sems)
    raw_x = (over_ctx, lambda p: raw_send.at[span(p, rows), :],
             lambda p: raw_recv.at[span(p, rows), :], raw_sems)
    grad_x = (over_ctx, lambda p: grad_send.at[span(p, rows), :],
              lambda p: grad_recv.at[span(p, rows), :], grad_sems)
    inner_x = (over_ctx, lambda p: inner_send.at[:, span(p, rows), :],
               lambda p: inner_recv.at[:, span(p, rows), :], inner_sems)
    slab_x = (over_ctx, lambda p: slab_send, lambda p: slab_recv.at[p], slab_sems)
    part_x = (over_chan, lambda p: part_send.at[span(p // x_count, part_rows), :],
              lambda p: part_recv.at[p], part_sems)
    sum_x = (over_ctx, lambda p: sum_send, lambda p: sum_recv.at[p], sum_sems)
    total_x = (over_z, lambda p: total_recv.at[span(my_z, part_rows), :],
               lambda p: total_recv.at[span(p, part_rows), :], total_sems)
    place_x = (over_chan, lambda p: place_send.at[span(p, rows), :], lambda p: place_recv.at[p], place_sems)
    spread_x = (over_chan, lambda p: place_sum,
                lambda p: place_all.at[span(p, rows), :], spread_sems)
    corner = (features + 7) // 8 * 8
    corner_rows = rows * LANES // hidden

    barrier = pltpu.get_barrier_semaphore()
    z_sides = [ahead(my_z, step, z_count) * x_count + my_x for step in (1, z_count - 1)]
    x_sides = [my_z * x_count + ahead(my_x, step, x_count) for step in (1, x_count - 1)]
    for step in ctx_steps:
        pl.semaphore_signal(barrier, inc=1, device_id=ctx_peer(step)[1],
                            device_id_type=pl.DeviceIdType.MESH)
    for side in z_sides + x_sides:
        pl.semaphore_signal(barrier, inc=1, device_id={"chan": side},
                            device_id_type=pl.DeviceIdType.MESH)

    round_sides = [z_sides] * (z_count // 2 - 1) + [x_sides] * (x_count // 2)

    def tell(num):
        for way, side in enumerate(round_sides[num]):
            pl.semaphore_signal(round_sems.at[num, way], inc=1, device_id={"chan": side},
                                device_id_type=pl.DeviceIdType.MESH)

    def hear(first, last):
        for num in range(first, min(last, len(round_sides))):
            for way in range(2):
                pl.semaphore_wait(round_sems.at[num, way], 1)
            if num + 1 < len(round_sides):
                tell(num + 1)

    for num in range(4):
        loads[num].wait()
    product = in_gate[...].astype(F32) * signal[...].astype(F32)
    through = grad_out[...].astype(F32) * out_gate[...].astype(F32)
    skip_part = jnp.sum(product * through, axis=1, keepdims=True)
    for row in range(rows):
        cut = slice(row * LANES, (row + 1) * LANES)
        pair_send[0, pl.ds(row, channels, stride=rows), :] = product[:, cut]
        pair_send[1, pl.ds(row, channels, stride=rows), :] = through[:, cut]

    for num in range(4, 10):
        loads[num].wait()
    pre_one = exact_dot(embed_weight[...], position_table[...], 0, 0)
    act_one, cos_one = sine_cosine(pre_one)
    pre_two = exact_dot(hidden_weight[...], act_one, 0, 0)
    act_two, cos_two = sine_cosine(pre_two)
    filter_halves = split(filter_weight[...])
    raw_filter = pair_dot(filter_halves, split(act_two), 1, 0)
    for row in range(rows):
        cut = slice(row * LANES, (row + 1) * LANES)
        raw_send[pl.ds(row, channels, stride=rows), :] = raw_filter[:, cut]

    pl.semaphore_wait(barrier, ctx_count + 3)
    tell(0)
    send(pair_x)
    send(raw_x)
    pair_recv[:, span(me, rows), :] = pair_send[:, span(me, rows), :]
    raw_recv[span(me, rows), :] = raw_send[span(me, rows), :]
    for num in range(10, INPUTS):
        loads[num].wait()

    keep_halves(act_one_keep, act_one)
    keep_halves(act_two_keep, act_two)
    keep_halves(position_keep, position_table[...])
    keep_halves(hidden_keep, hidden_weight[...])
    keep_halves(embed_keep, embed_weight[...])
    cos_one_keep[...] = cos_one
    cos_two_keep[...] = cos_two

    turn_cos = twist[0]
    turn_sin = twist[1]
    row_total = channels * rows

    def forward(fields):
        half = pair_dot(both(first_ref), split(jnp.concatenate(fields, axis=1)), 1, 0)
        turned = []
        for num in range(len(fields)):
            cut = slice(num * LANES, (num + 1) * LANES)
            real, imag = half[0:row_total, cut], half[row_total:, cut]
            turned.append(jnp.concatenate(
                [real * turn_cos + imag * turn_sin, imag * turn_cos - real * turn_sin], axis=1
            ))
        whole = pair_dot(split(jnp.concatenate(turned, axis=0)), both(second_ref), 1, 0)
        return [(whole[num * row_total:(num + 1) * row_total, 0:LANES],
                 whole[num * row_total:(num + 1) * row_total, LANES:]) for num in range(len(fields))]

    def times(first, second):
        real = first[0] * second[0] + first[1] * second[1]
        imag = first[0] * second[1] - first[1] * second[0]
        return jnp.concatenate([real, imag], axis=1)

    def inverse(spectra):
        half = pair_dot(split(jnp.concatenate(spectra, axis=0)), both(back_ref), 1, 0)
        turned = []
        for num in range(len(spectra)):
            cut = slice(num * row_total, (num + 1) * row_total)
            real, imag = half[cut, 0:LANES], half[cut, LANES:]
            turned.append(jnp.concatenate(
                [real * turn_cos - imag * turn_sin, real * turn_sin + imag * turn_cos], axis=0
            ))
        return pair_dot(both(last_ref), split(jnp.concatenate(turned, axis=1)), 1, 0)

    cells = (
        lax.broadcasted_iota(jnp.int32, (row_total, LANES), 0) * LANES
        + lax.broadcasted_iota(jnp.int32, (row_total, LANES), 1)
    ).astype(F32)
    envelope = jnp.exp(-decay[me] * cells)

    hear(0, 3)
    arrive(pair_x)
    own_product = pair_recv[0]
    own_through = pair_recv[1]
    product_spec, through_spec = forward([own_product, own_through])
    kernel_grad = inverse([times(product_spec, through_spec)])

    arrive(raw_x)
    shaped = raw_recv[...] * envelope
    energy = jnp.sum(jnp.sum(shaped * shaped, axis=0, keepdims=True), axis=1, keepdims=True)
    inverse_norm = lax.rsqrt(energy + EPSILON)
    filter_one = shaped * inverse_norm
    along = jnp.sum(jnp.sum(kernel_grad * filter_one, axis=0, keepdims=True), axis=1, keepdims=True)
    grad_send[...] = (kernel_grad - filter_one * along) * inverse_norm * envelope
    send(grad_x)
    grad_recv[span(me, rows), :] = grad_send[span(me, rows), :]

    (filter_spec,) = forward([filter_one])
    convs = inverse([
        times((filter_spec[0], -filter_spec[1]), product_spec), times(filter_spec, through_spec)
    ])
    inner_send[0] = convs[:, 0:LANES] + skip[me] * own_product
    inner_send[1] = convs[:, LANES:] + skip[me] * own_through
    send(inner_x)
    inner_recv[:, span(me, rows), :] = inner_send[:, span(me, rows), :]

    hear(3, len(round_sides))

    arrive(grad_x)
    raw_grad = jnp.concatenate(
        [grad_recv[pl.ds(row, channels, stride=rows), :] for row in range(rows)], axis=1
    )
    raw_grad_halves = split(raw_grad)
    pre_two_grad = pair_dot(filter_halves, raw_grad_halves, 0, 0) * cos_two_keep[...]
    pre_two_halves = split(pre_two_grad)
    pre_one_grad = pair_dot(both(hidden_keep), pre_two_halves, 1, 0) * cos_one_keep[...]
    pre_one_halves = split(pre_one_grad)
    part_send[...] = jnp.zeros_like(part_send)
    part_send[:, 0:hidden] = pair_dot(both(act_one_keep), pre_two_halves, 1, 1)
    part_send[0:features, hidden:2 * hidden] = pair_dot(
        both(position_keep), pre_one_halves, 1, 1
    )
    place = pair_dot(both(embed_keep), pre_one_halves, 1, 0)
    for num in range(corner_rows):
        part_send[corner + num:corner + num + 1, hidden:2 * hidden] = place[
            chan_count:features, num * hidden:(num + 1) * hidden
        ]
    send(part_x)
    part_recv[my_chan] = part_send[span(my_z, part_rows), :]
    for row in range(rows):
        place_send[pl.ds(row, chan_count, stride=rows), :] = place[
            0:chan_count, row * LANES:(row + 1) * LANES
        ]
    send(place_x)
    place_recv[my_chan] = place_send[span(my_chan, rows), :]
    slab_send[...] = jnp.broadcast_to(skip_part, (channels, LANES))
    slab_send[:, 0:hidden] = pair_dot(raw_grad_halves, both(act_two_keep), 1, 1)
    slab_recv[me] = slab_send[...]

    arrive(inner_x)
    for row in range(rows):
        cut = slice(row * LANES, (row + 1) * LANES)
        inner = inner_recv[0, pl.ds(row, channels, stride=rows), :]
        mixed[:, cut] = (out_gate[:, cut].astype(F32) * inner).astype(BF16)
        out_gate_grad[:, cut] = (grad_out[:, cut].astype(F32) * inner).astype(BF16)
        pull = inner_recv[1, pl.ds(row, channels, stride=rows), :]
        in_gate_grad[:, cut] = (pull * signal[:, cut].astype(F32)).astype(BF16)
        signal_grad[:, cut] = (pull * in_gate[:, cut].astype(F32)).astype(BF16)

    arrive(part_x)
    sum_send[...] = jnp.sum(part_recv[...], axis=0)
    send(sum_x)
    sum_recv[me] = sum_send[...]
    send(slab_x)

    arrive(place_x)
    place_sum[...] = jnp.sum(place_recv[...], axis=0)
    send(spread_x)
    place_all[span(my_chan, rows), :] = place_sum[...]

    arrive(sum_x)
    part_row = lax.broadcasted_iota(jnp.int32, (part_rows, LANES), 0) + my_z * part_rows
    part_lane = lax.broadcasted_iota(jnp.int32, (part_rows, LANES), 1)
    in_corner = (part_row >= corner) & (part_row < corner + corner_rows) & (part_lane >= hidden)
    total_recv[span(my_z, part_rows), :] = jnp.where(
        in_corner, sum_send[...], jnp.sum(sum_recv[...], axis=0) * scale
    )
    send(total_x)
    for exchange in (pair_x, raw_x, grad_x, inner_x, part_x, place_x, sum_x, slab_x):
        sent(exchange)

    arrive(slab_x)
    slab = jnp.sum(slab_recv[...], axis=0) * scale
    filter_grad[...] = slab[:, 0:hidden]
    picks = lax.broadcasted_iota(jnp.int32, (8, LANES), 1) == hidden
    skip_grad[...] = exact_dot(jnp.where(picks, 1.0, 0.0).astype(F32), slab, 1, 1)[0:1]

    arrive(spread_x)
    for row in range(rows):
        position_grad[0:chan_count, row * LANES:(row + 1) * LANES] = place_all[
            pl.ds(row, chan_count, stride=rows), :
        ]
    sent(spread_x)
    arrive(total_x)
    hidden_grad[...] = total_recv[:, 0:hidden]
    embed_grad[...] = total_recv[0:features, hidden:2 * hidden]
    for num in range(corner_rows):
        position_grad[chan_count:features, num * hidden:(num + 1) * hidden] = total_recv[
            corner + num:corner + num + 1, hidden:2 * hidden
        ]
    sent(total_x)


def put_out(*refs):
    count = len(refs) // 2
    copies = [
        pltpu.make_async_copy(refs[num], refs[count + num], refs[-1].at[num]) for num in range(count)
    ]
    for copy in copies:
        copy.start()
    for copy in copies:
        copy.wait()


def shards(
    x_count,
    out_gate,
    in_gate,
    signal,
    grad_out,
    position_table,
    embed_weight,
    hidden_weight,
    filter_weight,
    decay_rate,
    skip_gain,
):
    channels, length = signal.shape
    ctx_count = lax.axis_size("ctx")
    chan_count = lax.axis_size("chan")
    z_count = chan_count // x_count
    features, hidden = embed_weight.shape
    assert channels == ctx_count and length == z_count * LANES
    row_total = channels * z_count
    part_rows = hidden // z_count
    assert features == chan_count + 1 and 2 * hidden == LANES
    assert (features + 7) // 8 * 8 + length // hidden <= hidden
    vmem = pl.BlockSpec(memory_space=pltpu.VMEM)
    hbm = pl.BlockSpec(memory_space=pltpu.HBM)
    operands = (
        in_gate,
        signal,
        grad_out,
        out_gate,
        embed_weight,
        position_table,
        hidden_weight,
        filter_weight.T,
        decay_rate,
        skip_gain,
        *(jnp.asarray(table) for table in tables(row_total)),
    )
    block = jax.ShapeDtypeStruct((channels, length), BF16)
    shapes = (
        block,
        block,
        block,
        block,
        jax.ShapeDtypeStruct((features, hidden), F32),
        jax.ShapeDtypeStruct((hidden, hidden), F32),
        jax.ShapeDtypeStruct((channels, hidden), F32),
        jax.ShapeDtypeStruct((1, channels), F32),
        jax.ShapeDtypeStruct((features, length), F32),
    )
    scratch = [
        (pltpu.VMEM if operand.ndim > 1 else pltpu.SMEM)(operand.shape, operand.dtype)
        for operand in operands
    ]
    scratch += [
        pltpu.VMEM(shape, F32)
        for shape in (
            (2, row_total, LANES),
            (2, row_total, LANES),
            (row_total, LANES),
            (row_total, LANES),
            (row_total, LANES),
            (row_total, LANES),
            (2, row_total, LANES),
            (2, row_total, LANES),
            (channels, LANES),
            (ctx_count, channels, LANES),
            (hidden, LANES),
            (chan_count, part_rows, LANES),
            (part_rows, LANES),
            (ctx_count, part_rows, LANES),
            (hidden, LANES),
            (chan_count * z_count, LANES),
            (chan_count, z_count, LANES),
            (z_count, LANES),
            (chan_count * z_count, LANES),
        )
    ]
    scratch += [
        pltpu.VMEM((2,) + shape, BF16)
        for shape in (
            (hidden, length),
            (hidden, length),
            (features, length),
            (hidden, hidden),
            (features, hidden),
        )
    ]
    scratch += [pltpu.VMEM((hidden, length), F32)] * 2
    scratch += [pltpu.SemaphoreType.DMA((INPUTS,))]
    scratch += [
        pltpu.SemaphoreType.DMA((2, count))
        for count in [ctx_count] * 5 + [chan_count, ctx_count, z_count, chan_count, chan_count]
    ]
    scratch += [pltpu.SemaphoreType.REGULAR((z_count // 2 + x_count // 2, 2))]
    results = pl.pallas_call(
        functools.partial(kernel, ctx_count, z_count, x_count),
        out_shape=shapes,
        in_specs=[hbm] * INPUTS,
        out_specs=tuple([vmem] * 9),
        scratch_shapes=scratch,
        compiler_params=pltpu.CompilerParams(
            collective_id=0, has_side_effects=True, vmem_limit_bytes=40 * 1024 * 1024
        ),
    )(*(pltpu.with_memory_space_constraint(operand, pltpu.HBM) for operand in operands))
    results = pl.pallas_call(
        put_out,
        out_shape=tuple(pltpu.HBM(shape.shape, shape.dtype) for shape in shapes),
        in_specs=[vmem] * 9,
        out_specs=tuple([hbm] * 9),
        scratch_shapes=[pltpu.SemaphoreType.DMA((9,))],
        compiler_params=pltpu.CompilerParams(vmem_limit_bytes=4 * 1024 * 1024),
    )(*results)
    results = list(results)
    results[6] = results[6].T
    results[7] = results[7].reshape(channels)
    return tuple(results)


def solution(mesh, x_count=X_CHIPS):
    placed = (
        P("chan", "ctx"),
        P("chan", "ctx"),
        P("chan", "ctx"),
        P("chan", "ctx"),
        P(None, "ctx"),
        P(),
        P(),
        P(None, "chan"),
        P("chan"),
        P("chan"),
    )
    return jax.shard_map(
        functools.partial(shards, x_count),
        mesh=mesh,
        in_specs=placed,
        out_specs=(
            P("chan", "ctx"),
            P("chan", "ctx"),
            P("chan", "ctx"),
            P("chan", "ctx"),
            P(),
            P(),
            P(None, "chan"),
            P("chan"),
            P(None, "ctx"),
        ),
        check_vma=False,
    )
```

```python
import functools
import math

import jax
import jax.numpy as jnp
import ml_dtypes
import numpy as np
from jax import lax
from jax.experimental import pallas as pl
from jax.experimental.pallas import tpu as pltpu
from jax.sharding import PartitionSpec as P

EPSILON = 1e-06
F32 = jnp.float32
BF16 = jnp.bfloat16
LANES = 128
X_CHIPS = 4
INPUTS = 15
PI_HIGH = 3.140625
PI_MID = 9.67502593994140625e-4
PI_LOW = 1.509957990978376432e-7


def halves(table):
    high = table.astype(ml_dtypes.bfloat16)
    low = (table - high.astype(np.float64)).astype(ml_dtypes.bfloat16)
    return np.stack([high, low])


@functools.lru_cache(maxsize=None)
def tables(row_count):
    total = 2 * row_count * LANES
    ids = np.arange(row_count)
    lane_ids = np.arange(LANES)
    angle = 2 * np.pi * np.outer(ids + 0.5, ids) / (2 * row_count)
    first = np.concatenate([np.cos(angle), -np.sin(angle)], axis=0)
    last = first.T * (2.0 / total)
    lane_angle = 2 * np.pi * np.outer(lane_ids, lane_ids) / LANES
    cosine, sine = np.cos(lane_angle), np.sin(lane_angle)
    second = np.block([[cosine, -sine], [sine, cosine]])
    twist_angle = 2 * np.pi * np.outer(ids + 0.5, lane_ids) / total
    twist = np.stack([np.cos(twist_angle), np.sin(twist_angle)]).astype(np.float32)
    return halves(first), halves(last), halves(second), halves(second.T), twist


def exact_dot(left, right, left_dim, right_dim):
    return lax.dot_general(
        left,
        right,
        (((left_dim,), (right_dim,)), ((), ())),
        precision=lax.Precision.HIGHEST,
        preferred_element_type=F32,
    )


def split(value):
    high = value.astype(BF16)
    return high, (value - high.astype(F32)).astype(BF16)


def pair_dot(left, right, left_dim, right_dim):
    def one(first, second):
        return lax.dot_general(
            first, second, (((left_dim,), (right_dim,)), ((), ())), preferred_element_type=F32
        )

    return one(left[0], right[0]) + (one(left[0], right[1]) + one(left[1], right[0]))


def sine_cosine(angle):
    turns = jnp.floor(angle * (1.0 / math.pi) + 0.5)
    rest = ((angle - turns * PI_HIGH) - turns * PI_MID) - turns * PI_LOW
    odd = turns - 2.0 * jnp.floor(turns * 0.5)
    sign = 1.0 - 2.0 * odd
    square = rest * rest
    sine = 1.0 / math.factorial(13)
    for degree in (11, 9, 7, 5, 3, 1):
        sine = sine * square + (-1.0) ** (degree // 2) / math.factorial(degree)
    cosine = 1.0 / math.factorial(12)
    for degree in (10, 8, 6, 4, 2, 0):
        cosine = cosine * square + (-1.0) ** (degree // 2) / math.factorial(degree)
    return sine * (rest * sign), cosine * sign


def identity(size):
    rows = lax.broadcasted_iota(jnp.int32, (size, size), 0)
    cols = lax.broadcasted_iota(jnp.int32, (size, size), 1)
    return jnp.where(rows == cols, 1.0, 0.0).astype(F32)


def far_first(count):
    return sorted(range(1, count), key=lambda step: -min(step, count - step))


def kernel(ctx_count, z_count, x_count, *refs):
    sources, refs = refs[:INPUTS], refs[INPUTS:]
    (mixed, out_gate_grad, in_gate_grad, signal_grad, embed_grad, hidden_grad, filter_grad,
     skip_grad, position_grad), refs = refs[:9], refs[9:]
    locals_of, refs = refs[:INPUTS], refs[INPUTS:]
    (in_gate, signal, grad_out, out_gate, embed_weight, position_table, hidden_weight,
     filter_weight, decay, skip, first_ref, last_ref, second_ref, back_ref, twist) = locals_of
    (pair_send, pair_recv, raw_send, raw_recv, grad_send, grad_recv, inner_send, inner_recv,
     slab_send, slab_recv, part_send, part_recv, sum_send, sum_recv, total_recv,
     place_send, place_recv, place_sum, place_all, act_one_keep, act_two_keep, position_keep,
     hidden_keep, embed_keep, cos_one_keep, cos_two_keep), refs = refs[:26], refs[26:]
    (load_sems, pair_sems, raw_sems, grad_sems, inner_sems, slab_sems, part_sems, sum_sems,
     total_sems, place_sems, spread_sems, round_sems) = refs

    chan_count = z_count * x_count
    rows = z_count
    channels = ctx_count
    hidden = hidden_weight.shape[0]
    features = position_table.shape[0]
    part_rows = hidden // z_count
    me = lax.axis_index("ctx")
    my_chan = lax.axis_index("chan")
    my_z = my_chan // x_count
    my_x = my_chan % x_count
    scale = (ctx_count * rows * LANES) ** (-0.5)

    loads = {}
    for num, (source, local) in enumerate(zip(sources, locals_of)):
        loads[num] = pltpu.make_async_copy(source, local, load_sems.at[num])
        loads[num].start()

    def span(index, size):
        return pl.ds(pl.multiple_of(index * size, size), size)

    def ahead(index, step, count):
        index = index + step
        return jnp.where(index >= count, index - count, index) if step else index

    def ctx_peer(step):
        peer = ahead(me, step, ctx_count)
        return peer, {"ctx": peer}

    def chan_peer(step):
        z_step, x_step = step // x_count, step % x_count
        peer = ahead(my_z, z_step, z_count) * x_count + ahead(my_x, x_step, x_count)
        return peer, {"chan": peer}

    def z_peer(step):
        peer = ahead(my_z, step, z_count)
        return peer, {"chan": peer * x_count + my_x}

    def chan_far(step):
        z_step, x_step = step // x_count, step % x_count
        return -(min(z_step, z_count - z_step) + min(x_step, x_count - x_step))

    ctx_steps = far_first(ctx_count)
    z_steps = far_first(z_count)
    chan_steps = sorted(range(1, chan_count), key=chan_far)
    over_ctx = (ctx_peer, me, ctx_steps)
    over_chan = (chan_peer, my_chan, chan_steps)
    over_z = (z_peer, my_z, z_steps)

    def copy_of(exchange, step, slot):
        (peer_of, own, _), source, target, sems = exchange
        peer, device = peer_of(step)
        slot_index = own if slot == "own" else peer
        return pltpu.make_async_remote_copy(
            src_ref=source(peer),
            dst_ref=target(slot_index),
            send_sem=sems.at[0, step],
            recv_sem=sems.at[1, slot_index],
            device_id=device,
            device_id_type=pl.DeviceIdType.MESH,
        )

    def send(exchange):
        for step in exchange[0][2]:
            copy_of(exchange, step, "own").start()

    def arrive(exchange):
        for step in reversed(exchange[0][2]):
            copy_of(exchange, step, "peer").wait_recv()

    def sent(exchange):
        for step in exchange[0][2]:
            copy_of(exchange, step, "own").wait_send()

    def both(table):
        return table[0], table[1]

    def keep_halves(keep, value):
        keep[0], keep[1] = split(value)

    pair_x = (over_ctx, lambda p: pair_send.at[:, span(p, rows), :],
              lambda p: pair_recv.at[:, span(p, rows), :], pair_sems)
    raw_x = (over_ctx, lambda p: raw_send.at[span(p, rows), :],
             lambda p: raw_recv.at[span(p, rows), :], raw_sems)
    grad_x = (over_ctx, lambda p: grad_send.at[span(p, rows), :],
              lambda p: grad_recv.at[span(p, rows), :], grad_sems)
    inner_x = (over_ctx, lambda p: inner_send.at[:, span(p, rows), :],
               lambda p: inner_recv.at[:, span(p, rows), :], inner_sems)
    slab_x = (over_ctx, lambda p: slab_send, lambda p: slab_recv.at[p], slab_sems)
    part_x = (over_chan, lambda p: part_send.at[span(p // x_count, part_rows), :],
              lambda p: part_recv.at[p], part_sems)
    sum_x = (over_ctx, lambda p: sum_send, lambda p: sum_recv.at[p], sum_sems)
    total_x = (over_z, lambda p: total_recv.at[span(my_z, part_rows), :],
               lambda p: total_recv.at[span(p, part_rows), :], total_sems)
    place_x = (over_chan, lambda p: place_send.at[span(p, rows), :], lambda p: place_recv.at[p], place_sems)
    spread_x = (over_chan, lambda p: place_sum,
                lambda p: place_all.at[span(p, rows), :], spread_sems)
    corner = (features + 7) // 8 * 8
    corner_rows = rows * LANES // hidden

    barrier = pltpu.get_barrier_semaphore()

    def z_ways(*distances):
        ways = {way % z_count for far in distances for way in (far, -far)} - {0}
        return [ahead(my_z, way, z_count) * x_count + my_x for way in sorted(ways)]

    x_sides = [my_z * x_count + ahead(my_x, step, x_count) for step in range(1, x_count)]
    near_sides = z_ways(1, 2) + x_sides
    for step in ctx_steps:
        pl.semaphore_signal(barrier, inc=1, device_id=ctx_peer(step)[1],
                            device_id_type=pl.DeviceIdType.MESH)
    for side in near_sides:
        pl.semaphore_signal(barrier, inc=1, device_id={"chan": side},
                            device_id_type=pl.DeviceIdType.MESH)
    round_sides = [z_ways(2), x_sides]

    def tell(num):
        for way, side in enumerate(round_sides[num]):
            pl.semaphore_signal(round_sems.at[num, way], inc=1, device_id={"chan": side},
                                device_id_type=pl.DeviceIdType.MESH)

    def hear(first, last):
        for num in range(first, min(last, len(round_sides))):
            for way in range(len(round_sides[num])):
                pl.semaphore_wait(round_sems.at[num, way], 1)
            if num + 1 < len(round_sides):
                tell(num + 1)

    for num in range(4):
        loads[num].wait()
    product = in_gate[...].astype(F32) * signal[...].astype(F32)
    through = grad_out[...].astype(F32) * out_gate[...].astype(F32)
    skip_part = jnp.sum(product * through, axis=1, keepdims=True)
    for row in range(rows):
        cut = slice(row * LANES, (row + 1) * LANES)
        pair_send[0, pl.ds(row, channels, stride=rows), :] = product[:, cut]
        pair_send[1, pl.ds(row, channels, stride=rows), :] = through[:, cut]

    for num in range(4, 10):
        loads[num].wait()
    pre_one = exact_dot(embed_weight[...], position_table[...], 0, 0)
    act_one, cos_one = sine_cosine(pre_one)
    pre_two = exact_dot(hidden_weight[...], act_one, 0, 0)
    act_two, cos_two = sine_cosine(pre_two)
    filter_halves = split(filter_weight[...])
    raw_filter = pair_dot(filter_halves, split(act_two), 1, 0)
    for row in range(rows):
        cut = slice(row * LANES, (row + 1) * LANES)
        raw_send[pl.ds(row, channels, stride=rows), :] = raw_filter[:, cut]

    pl.semaphore_wait(barrier, ctx_count - 1 + len(near_sides))
    tell(0)
    send(pair_x)
    send(raw_x)
    pair_recv[:, span(me, rows), :] = pair_send[:, span(me, rows), :]
    raw_recv[span(me, rows), :] = raw_send[span(me, rows), :]
    for num in range(10, INPUTS):
        loads[num].wait()

    keep_halves(act_one_keep, act_one)
    keep_halves(act_two_keep, act_two)
    keep_halves(position_keep, position_table[...])
    keep_halves(hidden_keep, hidden_weight[...])
    keep_halves(embed_keep, embed_weight[...])
    cos_one_keep[...] = cos_one
    cos_two_keep[...] = cos_two

    turn_cos = twist[0]
    turn_sin = twist[1]
    row_total = channels * rows

    def forward(fields):
        half = pair_dot(both(first_ref), split(jnp.concatenate(fields, axis=1)), 1, 0)
        turned = []
        for num in range(len(fields)):
            cut = slice(num * LANES, (num + 1) * LANES)
            real, imag = half[0:row_total, cut], half[row_total:, cut]
            turned.append(jnp.concatenate(
                [real * turn_cos + imag * turn_sin, imag * turn_cos - real * turn_sin], axis=1
            ))
        whole = pair_dot(split(jnp.concatenate(turned, axis=0)), both(second_ref), 1, 0)
        return [(whole[num * row_total:(num + 1) * row_total, 0:LANES],
                 whole[num * row_total:(num + 1) * row_total, LANES:]) for num in range(len(fields))]

    def times(first, second):
        real = first[0] * second[0] + first[1] * second[1]
        imag = first[0] * second[1] - first[1] * second[0]
        return jnp.concatenate([real, imag], axis=1)

    def inverse(spectra):
        half = pair_dot(split(jnp.concatenate(spectra, axis=0)), both(back_ref), 1, 0)
        turned = []
        for num in range(len(spectra)):
            cut = slice(num * row_total, (num + 1) * row_total)
            real, imag = half[cut, 0:LANES], half[cut, LANES:]
            turned.append(jnp.concatenate(
                [real * turn_cos - imag * turn_sin, real * turn_sin + imag * turn_cos], axis=0
            ))
        return pair_dot(both(last_ref), split(jnp.concatenate(turned, axis=1)), 1, 0)

    cells = (
        lax.broadcasted_iota(jnp.int32, (row_total, LANES), 0) * LANES
        + lax.broadcasted_iota(jnp.int32, (row_total, LANES), 1)
    ).astype(F32)
    envelope = jnp.exp(-decay[me] * cells)

    hear(0, 2)
    arrive(pair_x)
    own_product = pair_recv[0]
    own_through = pair_recv[1]
    product_spec, through_spec = forward([own_product, own_through])
    kernel_grad = inverse([times(product_spec, through_spec)])

    arrive(raw_x)
    shaped = raw_recv[...] * envelope
    energy = jnp.sum(jnp.sum(shaped * shaped, axis=0, keepdims=True), axis=1, keepdims=True)
    inverse_norm = lax.rsqrt(energy + EPSILON)
    filter_one = shaped * inverse_norm
    along = jnp.sum(jnp.sum(kernel_grad * filter_one, axis=0, keepdims=True), axis=1, keepdims=True)
    grad_send[...] = (kernel_grad - filter_one * along) * inverse_norm * envelope
    send(grad_x)
    grad_recv[span(me, rows), :] = grad_send[span(me, rows), :]

    (filter_spec,) = forward([filter_one])
    convs = inverse([
        times((filter_spec[0], -filter_spec[1]), product_spec), times(filter_spec, through_spec)
    ])
    inner_send[0] = convs[:, 0:LANES] + skip[me] * own_product
    inner_send[1] = convs[:, LANES:] + skip[me] * own_through
    send(inner_x)
    inner_recv[:, span(me, rows), :] = inner_send[:, span(me, rows), :]

    hear(2, len(round_sides))

    arrive(grad_x)
    raw_grad = jnp.concatenate(
        [grad_recv[pl.ds(row, channels, stride=rows), :] for row in range(rows)], axis=1
    )
    raw_grad_halves = split(raw_grad)
    pre_two_grad = pair_dot(filter_halves, raw_grad_halves, 0, 0) * cos_two_keep[...]
    pre_two_halves = split(pre_two_grad)
    pre_one_grad = pair_dot(both(hidden_keep), pre_two_halves, 1, 0) * cos_one_keep[...]
    pre_one_halves = split(pre_one_grad)
    part_send[...] = jnp.zeros_like(part_send)
    part_send[:, 0:hidden] = pair_dot(both(act_one_keep), pre_two_halves, 1, 1)
    part_send[0:features, hidden:2 * hidden] = pair_dot(
        both(position_keep), pre_one_halves, 1, 1
    )
    place = pair_dot(both(embed_keep), pre_one_halves, 1, 0)
    for num in range(corner_rows):
        part_send[corner + num:corner + num + 1, hidden:2 * hidden] = place[
            chan_count:features, num * hidden:(num + 1) * hidden
        ]
    send(part_x)
    part_recv[my_chan] = part_send[span(my_z, part_rows), :]
    for row in range(rows):
        place_send[pl.ds(row, chan_count, stride=rows), :] = place[
            0:chan_count, row * LANES:(row + 1) * LANES
        ]
    send(place_x)
    place_recv[my_chan] = place_send[span(my_chan, rows), :]
    slab_send[...] = jnp.broadcast_to(skip_part, (channels, LANES))
    slab_send[:, 0:hidden] = pair_dot(raw_grad_halves, both(act_two_keep), 1, 1)
    slab_recv[me] = slab_send[...]
    send(slab_x)

    arrive(inner_x)
    for row in range(rows):
        cut = slice(row * LANES, (row + 1) * LANES)
        inner = inner_recv[0, pl.ds(row, channels, stride=rows), :]
        mixed[:, cut] = (out_gate[:, cut].astype(F32) * inner).astype(BF16)
        out_gate_grad[:, cut] = (grad_out[:, cut].astype(F32) * inner).astype(BF16)
        pull = inner_recv[1, pl.ds(row, channels, stride=rows), :]
        in_gate_grad[:, cut] = (pull * signal[:, cut].astype(F32)).astype(BF16)
        signal_grad[:, cut] = (pull * in_gate[:, cut].astype(F32)).astype(BF16)

    arrive(part_x)
    sum_send[...] = jnp.sum(part_recv[...], axis=0)
    send(sum_x)
    sum_recv[me] = sum_send[...]

    arrive(place_x)
    place_sum[...] = jnp.sum(place_recv[...], axis=0)
    send(spread_x)
    place_all[span(my_chan, rows), :] = place_sum[...]

    arrive(sum_x)
    part_row = lax.broadcasted_iota(jnp.int32, (part_rows, LANES), 0) + my_z * part_rows
    part_lane = lax.broadcasted_iota(jnp.int32, (part_rows, LANES), 1)
    in_corner = (part_row >= corner) & (part_row < corner + corner_rows) & (part_lane >= hidden)
    total_recv[span(my_z, part_rows), :] = jnp.where(
        in_corner, sum_send[...], jnp.sum(sum_recv[...], axis=0) * scale
    )
    send(total_x)
    for exchange in (pair_x, raw_x, grad_x, inner_x, part_x, place_x, sum_x, slab_x):
        sent(exchange)

    arrive(slab_x)
    slab = jnp.sum(slab_recv[...], axis=0) * scale
    filter_grad[...] = slab[:, 0:hidden]
    picks = lax.broadcasted_iota(jnp.int32, (8, LANES), 1) == hidden
    skip_grad[...] = exact_dot(jnp.where(picks, 1.0, 0.0).astype(F32), slab, 1, 1)[0:1]

    arrive(spread_x)
    for row in range(rows):
        position_grad[0:chan_count, row * LANES:(row + 1) * LANES] = place_all[
            pl.ds(row, chan_count, stride=rows), :
        ]
    sent(spread_x)
    arrive(total_x)
    hidden_grad[...] = total_recv[:, 0:hidden]
    embed_grad[...] = total_recv[0:features, hidden:2 * hidden]
    for num in range(corner_rows):
        position_grad[chan_count:features, num * hidden:(num + 1) * hidden] = total_recv[
            corner + num:corner + num + 1, hidden:2 * hidden
        ]
    sent(total_x)


def put_out(*refs):
    count = len(refs) // 2
    copies = [
        pltpu.make_async_copy(refs[num], refs[count + num], refs[-1].at[num]) for num in range(count)
    ]
    for copy in copies:
        copy.start()
    for copy in copies:
        copy.wait()


def shards(
    x_count,
    out_gate,
    in_gate,
    signal,
    grad_out,
    position_table,
    embed_weight,
    hidden_weight,
    filter_weight,
    decay_rate,
    skip_gain,
):
    channels, length = signal.shape
    ctx_count = lax.axis_size("ctx")
    chan_count = lax.axis_size("chan")
    z_count = chan_count // x_count
    features, hidden = embed_weight.shape
    assert channels == ctx_count and length == z_count * LANES
    row_total = channels * z_count
    part_rows = hidden // z_count
    assert features == chan_count + 1 and 2 * hidden == LANES
    assert (features + 7) // 8 * 8 + length // hidden <= hidden
    vmem = pl.BlockSpec(memory_space=pltpu.VMEM)
    hbm = pl.BlockSpec(memory_space=pltpu.HBM)
    operands = (
        in_gate,
        signal,
        grad_out,
        out_gate,
        embed_weight,
        position_table,
        hidden_weight,
        filter_weight.T,
        decay_rate,
        skip_gain,
        *(jnp.asarray(table) for table in tables(row_total)),
    )
    block = jax.ShapeDtypeStruct((channels, length), BF16)
    shapes = (
        block,
        block,
        block,
        block,
        jax.ShapeDtypeStruct((features, hidden), F32),
        jax.ShapeDtypeStruct((hidden, hidden), F32),
        jax.ShapeDtypeStruct((channels, hidden), F32),
        jax.ShapeDtypeStruct((1, channels), F32),
        jax.ShapeDtypeStruct((features, length), F32),
    )
    scratch = [
        (pltpu.VMEM if operand.ndim > 1 else pltpu.SMEM)(operand.shape, operand.dtype)
        for operand in operands
    ]
    scratch += [
        pltpu.VMEM(shape, F32)
        for shape in (
            (2, row_total, LANES),
            (2, row_total, LANES),
            (row_total, LANES),
            (row_total, LANES),
            (row_total, LANES),
            (row_total, LANES),
            (2, row_total, LANES),
            (2, row_total, LANES),
            (channels, LANES),
            (ctx_count, channels, LANES),
            (hidden, LANES),
            (chan_count, part_rows, LANES),
            (part_rows, LANES),
            (ctx_count, part_rows, LANES),
            (hidden, LANES),
            (chan_count * z_count, LANES),
            (chan_count, z_count, LANES),
            (z_count, LANES),
            (chan_count * z_count, LANES),
        )
    ]
    scratch += [
        pltpu.VMEM((2,) + shape, BF16)
        for shape in (
            (hidden, length),
            (hidden, length),
            (features, length),
            (hidden, hidden),
            (features, hidden),
        )
    ]
    scratch += [pltpu.VMEM((hidden, length), F32)] * 2
    scratch += [pltpu.SemaphoreType.DMA((INPUTS,))]
    scratch += [
        pltpu.SemaphoreType.DMA((2, count))
        for count in [ctx_count] * 5 + [chan_count, ctx_count, z_count, chan_count, chan_count]
    ]
    scratch += [pltpu.SemaphoreType.REGULAR((4, max(4, x_count)))]
    results = pl.pallas_call(
        functools.partial(kernel, ctx_count, z_count, x_count),
        out_shape=shapes,
        in_specs=[hbm] * INPUTS,
        out_specs=tuple([vmem] * 9),
        scratch_shapes=scratch,
        compiler_params=pltpu.CompilerParams(
            collective_id=0, has_side_effects=True, vmem_limit_bytes=40 * 1024 * 1024
        ),
    )(*(pltpu.with_memory_space_constraint(operand, pltpu.HBM) for operand in operands))
    results = pl.pallas_call(
        put_out,
        out_shape=tuple(pltpu.HBM(shape.shape, shape.dtype) for shape in shapes),
        in_specs=[vmem] * 9,
        out_specs=tuple([hbm] * 9),
        scratch_shapes=[pltpu.SemaphoreType.DMA((9,))],
        compiler_params=pltpu.CompilerParams(vmem_limit_bytes=4 * 1024 * 1024),
    )(*results)
    results = list(results)
    results[6] = results[6].T
    results[7] = results[7].reshape(channels)
    return tuple(results)


def solution(mesh, x_count=X_CHIPS):
    placed = (
        P("chan", "ctx"),
        P("chan", "ctx"),
        P("chan", "ctx"),
        P("chan", "ctx"),
        P(None, "ctx"),
        P(),
        P(),
        P(None, "chan"),
        P("chan"),
        P("chan"),
    )
    return jax.shard_map(
        functools.partial(shards, x_count),
        mesh=mesh,
        in_specs=placed,
        out_specs=(
            P("chan", "ctx"),
            P("chan", "ctx"),
            P("chan", "ctx"),
            P("chan", "ctx"),
            P(),
            P(),
            P(None, "chan"),
            P("chan"),
            P(None, "ctx"),
        ),
        check_vma=False,
    )
```

```python
import functools
import math

import jax
import jax.numpy as jnp
import ml_dtypes
import numpy as np
from jax import lax
from jax.experimental import pallas as pl
from jax.experimental.pallas import tpu as pltpu
from jax.sharding import PartitionSpec as P

EPSILON = 1e-06
F32 = jnp.float32
BF16 = jnp.bfloat16
LANES = 128
X_CHIPS = 4
INPUTS = 15
PI_HIGH = 3.140625
PI_MID = 9.67502593994140625e-4
PI_LOW = 1.509957990978376432e-7


def halves(table):
    high = table.astype(ml_dtypes.bfloat16)
    low = (table - high.astype(np.float64)).astype(ml_dtypes.bfloat16)
    return np.stack([high, low])


@functools.lru_cache(maxsize=None)
def tables(row_count):
    total = 2 * row_count * LANES
    ids = np.arange(row_count)
    lane_ids = np.arange(LANES)
    angle = 2 * np.pi * np.outer(ids + 0.5, ids) / (2 * row_count)
    first = np.concatenate([np.cos(angle), -np.sin(angle)], axis=0)
    last = first.T * (2.0 / total)
    lane_angle = 2 * np.pi * np.outer(lane_ids, lane_ids) / LANES
    cosine, sine = np.cos(lane_angle), np.sin(lane_angle)
    second = np.block([[cosine, -sine], [sine, cosine]])
    twist_angle = 2 * np.pi * np.outer(ids + 0.5, lane_ids) / total
    twist = np.stack([np.cos(twist_angle), np.sin(twist_angle)]).astype(np.float32)
    return halves(first), halves(last), halves(second), halves(second.T), twist


def exact_dot(left, right, left_dim, right_dim):
    return lax.dot_general(
        left,
        right,
        (((left_dim,), (right_dim,)), ((), ())),
        precision=lax.Precision.HIGHEST,
        preferred_element_type=F32,
    )


def split(value):
    high = value.astype(BF16)
    return high, (value - high.astype(F32)).astype(BF16)


def pair_dot(left, right, left_dim, right_dim):
    def one(first, second):
        return lax.dot_general(
            first, second, (((left_dim,), (right_dim,)), ((), ())), preferred_element_type=F32
        )

    return one(left[0], right[0]) + (one(left[0], right[1]) + one(left[1], right[0]))


def sine_cosine(angle):
    turns = jnp.floor(angle * (1.0 / math.pi) + 0.5)
    rest = ((angle - turns * PI_HIGH) - turns * PI_MID) - turns * PI_LOW
    odd = turns - 2.0 * jnp.floor(turns * 0.5)
    sign = 1.0 - 2.0 * odd
    square = rest * rest
    sine = 1.0 / math.factorial(13)
    for degree in (11, 9, 7, 5, 3, 1):
        sine = sine * square + (-1.0) ** (degree // 2) / math.factorial(degree)
    cosine = 1.0 / math.factorial(12)
    for degree in (10, 8, 6, 4, 2, 0):
        cosine = cosine * square + (-1.0) ** (degree // 2) / math.factorial(degree)
    return sine * (rest * sign), cosine * sign


def identity(size):
    rows = lax.broadcasted_iota(jnp.int32, (size, size), 0)
    cols = lax.broadcasted_iota(jnp.int32, (size, size), 1)
    return jnp.where(rows == cols, 1.0, 0.0).astype(F32)


def far_first(count):
    return sorted(range(1, count), key=lambda step: -min(step, count - step))


def kernel(ctx_count, z_count, x_count, *refs):
    sources, refs = refs[:INPUTS], refs[INPUTS:]
    (mixed, out_gate_grad, in_gate_grad, signal_grad, embed_grad, hidden_grad, filter_grad,
     skip_grad, position_grad), refs = refs[:9], refs[9:]
    locals_of, refs = refs[:INPUTS], refs[INPUTS:]
    (in_gate, signal, grad_out, out_gate, embed_weight, position_table, hidden_weight,
     filter_weight, decay, skip, first_ref, last_ref, second_ref, back_ref, twist) = locals_of
    (pair_send, pair_recv, raw_send, raw_recv, grad_send, grad_recv, inner_send, inner_recv,
     slab_send, slab_recv, part_send, part_recv, sum_send, sum_recv, total_recv,
     place_send, place_recv, place_sum, place_all, act_one_keep, act_two_keep, position_keep,
     hidden_keep, embed_keep, cos_one_keep, cos_two_keep), refs = refs[:26], refs[26:]
    (load_sems, pair_sems, raw_sems, grad_sems, inner_sems, slab_sems, part_sems, sum_sems,
     total_sems, place_sems, spread_sems, round_sems) = refs

    chan_count = z_count * x_count
    rows = z_count
    channels = ctx_count
    hidden = hidden_weight.shape[0]
    features = position_table.shape[0]
    part_rows = hidden // z_count
    me = lax.axis_index("ctx")
    my_chan = lax.axis_index("chan")
    my_z = my_chan // x_count
    my_x = my_chan % x_count
    scale = (ctx_count * rows * LANES) ** (-0.5)

    loads = {}
    for num, (source, local) in enumerate(zip(sources, locals_of)):
        loads[num] = pltpu.make_async_copy(source, local, load_sems.at[num])
        loads[num].start()

    def span(index, size):
        return pl.ds(pl.multiple_of(index * size, size), size)

    def ahead(index, step, count):
        index = index + step
        return jnp.where(index >= count, index - count, index) if step else index

    def ctx_peer(step):
        peer = ahead(me, step, ctx_count)
        return peer, {"ctx": peer}

    def chan_peer(step):
        z_step, x_step = step // x_count, step % x_count
        peer = ahead(my_z, z_step, z_count) * x_count + ahead(my_x, x_step, x_count)
        return peer, {"chan": peer}

    def z_peer(step):
        peer = ahead(my_z, step, z_count)
        return peer, {"chan": peer * x_count + my_x}

    def chan_far(step):
        z_step, x_step = step // x_count, step % x_count
        return -(min(z_step, z_count - z_step) + min(x_step, x_count - x_step))

    ctx_steps = far_first(ctx_count)
    z_steps = far_first(z_count)
    chan_steps = sorted(
        range(1, chan_count),
        key=lambda step: (-min(step // x_count, z_count - step // x_count), chan_far(step)),
    )
    over_ctx = (ctx_peer, me, ctx_steps)
    over_chan = (chan_peer, my_chan, chan_steps)
    over_z = (z_peer, my_z, z_steps)

    def copy_of(exchange, step, slot):
        (peer_of, own, _), source, target, sems = exchange
        peer, device = peer_of(step)
        slot_index = own if slot == "own" else peer
        return pltpu.make_async_remote_copy(
            src_ref=source(peer),
            dst_ref=target(slot_index),
            send_sem=sems.at[0, step],
            recv_sem=sems.at[1, slot_index],
            device_id=device,
            device_id_type=pl.DeviceIdType.MESH,
        )

    def send(exchange):
        for step in exchange[0][2]:
            copy_of(exchange, step, "own").start()

    def arrive(exchange):
        for step in reversed(exchange[0][2]):
            copy_of(exchange, step, "peer").wait_recv()

    def sent(exchange):
        for step in exchange[0][2]:
            copy_of(exchange, step, "own").wait_send()

    def both(table):
        return table[0], table[1]

    def keep_halves(keep, value):
        keep[0], keep[1] = split(value)

    pair_x = (over_ctx, lambda p: pair_send.at[:, span(p, rows), :],
              lambda p: pair_recv.at[:, span(p, rows), :], pair_sems)
    raw_x = (over_ctx, lambda p: raw_send.at[span(p, rows), :],
             lambda p: raw_recv.at[span(p, rows), :], raw_sems)
    grad_x = (over_ctx, lambda p: grad_send.at[span(p, rows), :],
              lambda p: grad_recv.at[span(p, rows), :], grad_sems)
    inner_x = (over_ctx, lambda p: inner_send.at[:, span(p, rows), :],
               lambda p: inner_recv.at[:, span(p, rows), :], inner_sems)
    slab_x = (over_ctx, lambda p: slab_send, lambda p: slab_recv.at[p], slab_sems)
    part_x = (over_chan, lambda p: part_send.at[span(p // x_count, part_rows), :],
              lambda p: part_recv.at[p], part_sems)
    sum_x = (over_ctx, lambda p: sum_send, lambda p: sum_recv.at[p], sum_sems)
    total_x = (over_z, lambda p: total_recv.at[span(my_z, part_rows), :],
               lambda p: total_recv.at[span(p, part_rows), :], total_sems)
    place_x = (over_chan, lambda p: place_send.at[span(p, rows), :], lambda p: place_recv.at[p], place_sems)
    spread_x = (over_chan, lambda p: place_sum,
                lambda p: place_all.at[span(p, rows), :], spread_sems)
    corner = (features + 7) // 8 * 8
    corner_rows = rows * LANES // hidden

    barrier = pltpu.get_barrier_semaphore()

    def z_ways(*distances):
        ways = {way % z_count for far in distances for way in (far, -far)} - {0}
        return [ahead(my_z, way, z_count) * x_count + my_x for way in sorted(ways)]

    x_sides = [my_z * x_count + ahead(my_x, step, x_count) for step in range(1, x_count)]
    near_sides = z_ways(1, 2) + x_sides
    for step in ctx_steps:
        pl.semaphore_signal(barrier, inc=1, device_id=ctx_peer(step)[1],
                            device_id_type=pl.DeviceIdType.MESH)
    for side in near_sides:
        pl.semaphore_signal(barrier, inc=1, device_id={"chan": side},
                            device_id_type=pl.DeviceIdType.MESH)
    round_sides = [z_ways(2), x_sides]

    def tell(num):
        for way, side in enumerate(round_sides[num]):
            pl.semaphore_signal(round_sems.at[num, way], inc=1, device_id={"chan": side},
                                device_id_type=pl.DeviceIdType.MESH)

    def hear(first, last):
        for num in range(first, min(last, len(round_sides))):
            for way in range(len(round_sides[num])):
                pl.semaphore_wait(round_sems.at[num, way], 1)
            if num + 1 < len(round_sides):
                tell(num + 1)

    for num in range(4):
        loads[num].wait()
    product = in_gate[...].astype(F32) * signal[...].astype(F32)
    through = grad_out[...].astype(F32) * out_gate[...].astype(F32)
    skip_part = jnp.sum(product * through, axis=1, keepdims=True)
    for row in range(rows):
        cut = slice(row * LANES, (row + 1) * LANES)
        pair_send[0, pl.ds(row, channels, stride=rows), :] = product[:, cut]
        pair_send[1, pl.ds(row, channels, stride=rows), :] = through[:, cut]

    for num in range(4, 10):
        loads[num].wait()
    pre_one = exact_dot(embed_weight[...], position_table[...], 0, 0)
    act_one, cos_one = sine_cosine(pre_one)
    pre_two = exact_dot(hidden_weight[...], act_one, 0, 0)
    act_two, cos_two = sine_cosine(pre_two)
    filter_halves = split(filter_weight[...])
    raw_filter = pair_dot(filter_halves, split(act_two), 1, 0)
    for row in range(rows):
        cut = slice(row * LANES, (row + 1) * LANES)
        raw_send[pl.ds(row, channels, stride=rows), :] = raw_filter[:, cut]

    pl.semaphore_wait(barrier, ctx_count - 1 + len(near_sides))
    tell(0)
    send(pair_x)
    send(raw_x)
    pair_recv[:, span(me, rows), :] = pair_send[:, span(me, rows), :]
    raw_recv[span(me, rows), :] = raw_send[span(me, rows), :]
    for num in range(10, INPUTS):
        loads[num].wait()

    keep_halves(act_one_keep, act_one)
    keep_halves(act_two_keep, act_two)
    keep_halves(position_keep, position_table[...])
    keep_halves(hidden_keep, hidden_weight[...])
    keep_halves(embed_keep, embed_weight[...])
    cos_one_keep[...] = cos_one
    cos_two_keep[...] = cos_two

    turn_cos = twist[0]
    turn_sin = twist[1]
    row_total = channels * rows

    def forward(fields):
        half = pair_dot(both(first_ref), split(jnp.concatenate(fields, axis=1)), 1, 0)
        turned = []
        for num in range(len(fields)):
            cut = slice(num * LANES, (num + 1) * LANES)
            real, imag = half[0:row_total, cut], half[row_total:, cut]
            turned.append(jnp.concatenate(
                [real * turn_cos + imag * turn_sin, imag * turn_cos - real * turn_sin], axis=1
            ))
        whole = pair_dot(split(jnp.concatenate(turned, axis=0)), both(second_ref), 1, 0)
        return [(whole[num * row_total:(num + 1) * row_total, 0:LANES],
                 whole[num * row_total:(num + 1) * row_total, LANES:]) for num in range(len(fields))]

    def times(first, second):
        real = first[0] * second[0] + first[1] * second[1]
        imag = first[0] * second[1] - first[1] * second[0]
        return jnp.concatenate([real, imag], axis=1)

    def inverse(spectra):
        half = pair_dot(split(jnp.concatenate(spectra, axis=0)), both(back_ref), 1, 0)
        turned = []
        for num in range(len(spectra)):
            cut = slice(num * row_total, (num + 1) * row_total)
            real, imag = half[cut, 0:LANES], half[cut, LANES:]
            turned.append(jnp.concatenate(
                [real * turn_cos - imag * turn_sin, real * turn_sin + imag * turn_cos], axis=0
            ))
        return pair_dot(both(last_ref), split(jnp.concatenate(turned, axis=1)), 1, 0)

    cells = (
        lax.broadcasted_iota(jnp.int32, (row_total, LANES), 0) * LANES
        + lax.broadcasted_iota(jnp.int32, (row_total, LANES), 1)
    ).astype(F32)
    envelope = jnp.exp(-decay[me] * cells)

    hear(0, 2)
    arrive(pair_x)
    own_product = pair_recv[0]
    own_through = pair_recv[1]
    product_spec, through_spec = forward([own_product, own_through])
    kernel_grad = inverse([times(product_spec, through_spec)])

    arrive(raw_x)
    shaped = raw_recv[...] * envelope
    energy = jnp.sum(jnp.sum(shaped * shaped, axis=0, keepdims=True), axis=1, keepdims=True)
    inverse_norm = lax.rsqrt(energy + EPSILON)
    filter_one = shaped * inverse_norm
    along = jnp.sum(jnp.sum(kernel_grad * filter_one, axis=0, keepdims=True), axis=1, keepdims=True)
    grad_send[...] = (kernel_grad - filter_one * along) * inverse_norm * envelope
    send(grad_x)
    grad_recv[span(me, rows), :] = grad_send[span(me, rows), :]

    (filter_spec,) = forward([filter_one])
    convs = inverse([
        times((filter_spec[0], -filter_spec[1]), product_spec), times(filter_spec, through_spec)
    ])
    inner_send[0] = convs[:, 0:LANES] + skip[me] * own_product
    inner_send[1] = convs[:, LANES:] + skip[me] * own_through
    send(inner_x)
    inner_recv[:, span(me, rows), :] = inner_send[:, span(me, rows), :]

    hear(2, len(round_sides))

    arrive(grad_x)
    raw_grad = jnp.concatenate(
        [grad_recv[pl.ds(row, channels, stride=rows), :] for row in range(rows)], axis=1
    )
    raw_grad_halves = split(raw_grad)
    pre_two_grad = pair_dot(filter_halves, raw_grad_halves, 0, 0) * cos_two_keep[...]
    pre_two_halves = split(pre_two_grad)
    pre_one_grad = pair_dot(both(hidden_keep), pre_two_halves, 1, 0) * cos_one_keep[...]
    pre_one_halves = split(pre_one_grad)
    part_send[...] = jnp.zeros_like(part_send)
    part_send[:, 0:hidden] = pair_dot(both(act_one_keep), pre_two_halves, 1, 1)
    part_send[0:features, hidden:2 * hidden] = pair_dot(
        both(position_keep), pre_one_halves, 1, 1
    )
    place = pair_dot(both(embed_keep), pre_one_halves, 1, 0)
    for num in range(corner_rows):
        part_send[corner + num:corner + num + 1, hidden:2 * hidden] = place[
            chan_count:features, num * hidden:(num + 1) * hidden
        ]
    send(part_x)
    part_recv[my_chan] = part_send[span(my_z, part_rows), :]
    for row in range(rows):
        place_send[pl.ds(row, chan_count, stride=rows), :] = place[
            0:chan_count, row * LANES:(row + 1) * LANES
        ]
    send(place_x)
    place_recv[my_chan] = place_send[span(my_chan, rows), :]
    slab_send[...] = jnp.broadcast_to(skip_part, (channels, LANES))
    slab_send[:, 0:hidden] = pair_dot(raw_grad_halves, both(act_two_keep), 1, 1)
    slab_recv[me] = slab_send[...]
    send(slab_x)

    arrive(inner_x)
    for row in range(rows):
        cut = slice(row * LANES, (row + 1) * LANES)
        inner = inner_recv[0, pl.ds(row, channels, stride=rows), :]
        mixed[:, cut] = (out_gate[:, cut].astype(F32) * inner).astype(BF16)
        out_gate_grad[:, cut] = (grad_out[:, cut].astype(F32) * inner).astype(BF16)
        pull = inner_recv[1, pl.ds(row, channels, stride=rows), :]
        in_gate_grad[:, cut] = (pull * signal[:, cut].astype(F32)).astype(BF16)
        signal_grad[:, cut] = (pull * in_gate[:, cut].astype(F32)).astype(BF16)

    arrive(part_x)
    sum_send[...] = jnp.sum(part_recv[...], axis=0)
    send(sum_x)
    sum_recv[me] = sum_send[...]

    arrive(place_x)
    place_sum[...] = jnp.sum(place_recv[...], axis=0)
    send(spread_x)
    place_all[span(my_chan, rows), :] = place_sum[...]

    arrive(sum_x)
    part_row = lax.broadcasted_iota(jnp.int32, (part_rows, LANES), 0) + my_z * part_rows
    part_lane = lax.broadcasted_iota(jnp.int32, (part_rows, LANES), 1)
    in_corner = (part_row >= corner) & (part_row < corner + corner_rows) & (part_lane >= hidden)
    total_recv[span(my_z, part_rows), :] = jnp.where(
        in_corner, sum_send[...], jnp.sum(sum_recv[...], axis=0) * scale
    )
    send(total_x)
    for exchange in (pair_x, raw_x, grad_x, inner_x, part_x, place_x, sum_x, slab_x):
        sent(exchange)

    arrive(slab_x)
    slab = jnp.sum(slab_recv[...], axis=0) * scale
    filter_grad[...] = slab[:, 0:hidden]
    picks = lax.broadcasted_iota(jnp.int32, (8, LANES), 1) == hidden
    skip_grad[...] = exact_dot(jnp.where(picks, 1.0, 0.0).astype(F32), slab, 1, 1)[0:1]

    arrive(spread_x)
    for row in range(rows):
        position_grad[0:chan_count, row * LANES:(row + 1) * LANES] = place_all[
            pl.ds(row, chan_count, stride=rows), :
        ]
    sent(spread_x)
    arrive(total_x)
    hidden_grad[...] = total_recv[:, 0:hidden]
    embed_grad[...] = total_recv[0:features, hidden:2 * hidden]
    for num in range(corner_rows):
        position_grad[chan_count:features, num * hidden:(num + 1) * hidden] = total_recv[
            corner + num:corner + num + 1, hidden:2 * hidden
        ]
    sent(total_x)


def put_out(*refs):
    count = len(refs) // 2
    copies = [
        pltpu.make_async_copy(refs[num], refs[count + num], refs[-1].at[num]) for num in range(count)
    ]
    for copy in copies:
        copy.start()
    for copy in copies:
        copy.wait()


def shards(
    x_count,
    out_gate,
    in_gate,
    signal,
    grad_out,
    position_table,
    embed_weight,
    hidden_weight,
    filter_weight,
    decay_rate,
    skip_gain,
):
    channels, length = signal.shape
    ctx_count = lax.axis_size("ctx")
    chan_count = lax.axis_size("chan")
    z_count = chan_count // x_count
    features, hidden = embed_weight.shape
    assert channels == ctx_count and length == z_count * LANES
    row_total = channels * z_count
    part_rows = hidden // z_count
    assert features == chan_count + 1 and 2 * hidden == LANES
    assert (features + 7) // 8 * 8 + length // hidden <= hidden
    vmem = pl.BlockSpec(memory_space=pltpu.VMEM)
    hbm = pl.BlockSpec(memory_space=pltpu.HBM)
    operands = (
        in_gate,
        signal,
        grad_out,
        out_gate,
        embed_weight,
        position_table,
        hidden_weight,
        filter_weight.T,
        decay_rate,
        skip_gain,
        *(jnp.asarray(table) for table in tables(row_total)),
    )
    block = jax.ShapeDtypeStruct((channels, length), BF16)
    shapes = (
        block,
        block,
        block,
        block,
        jax.ShapeDtypeStruct((features, hidden), F32),
        jax.ShapeDtypeStruct((hidden, hidden), F32),
        jax.ShapeDtypeStruct((channels, hidden), F32),
        jax.ShapeDtypeStruct((1, channels), F32),
        jax.ShapeDtypeStruct((features, length), F32),
    )
    scratch = [
        (pltpu.VMEM if operand.ndim > 1 else pltpu.SMEM)(operand.shape, operand.dtype)
        for operand in operands
    ]
    scratch += [
        pltpu.VMEM(shape, F32)
        for shape in (
            (2, row_total, LANES),
            (2, row_total, LANES),
            (row_total, LANES),
            (row_total, LANES),
            (row_total, LANES),
            (row_total, LANES),
            (2, row_total, LANES),
            (2, row_total, LANES),
            (channels, LANES),
            (ctx_count, channels, LANES),
            (hidden, LANES),
            (chan_count, part_rows, LANES),
            (part_rows, LANES),
            (ctx_count, part_rows, LANES),
            (hidden, LANES),
            (chan_count * z_count, LANES),
            (chan_count, z_count, LANES),
            (z_count, LANES),
            (chan_count * z_count, LANES),
        )
    ]
    scratch += [
        pltpu.VMEM((2,) + shape, BF16)
        for shape in (
            (hidden, length),
            (hidden, length),
            (features, length),
            (hidden, hidden),
            (features, hidden),
        )
    ]
    scratch += [pltpu.VMEM((hidden, length), F32)] * 2
    scratch += [pltpu.SemaphoreType.DMA((INPUTS,))]
    scratch += [
        pltpu.SemaphoreType.DMA((2, count))
        for count in [ctx_count] * 5 + [chan_count, ctx_count, z_count, chan_count, chan_count]
    ]
    scratch += [pltpu.SemaphoreType.REGULAR((4, max(4, x_count)))]
    results = pl.pallas_call(
        functools.partial(kernel, ctx_count, z_count, x_count),
        out_shape=shapes,
        in_specs=[hbm] * INPUTS,
        out_specs=tuple([vmem] * 9),
        scratch_shapes=scratch,
        compiler_params=pltpu.CompilerParams(
            collective_id=0, has_side_effects=True, vmem_limit_bytes=40 * 1024 * 1024
        ),
    )(*(pltpu.with_memory_space_constraint(operand, pltpu.HBM) for operand in operands))
    results = pl.pallas_call(
        put_out,
        out_shape=tuple(pltpu.HBM(shape.shape, shape.dtype) for shape in shapes),
        in_specs=[vmem] * 9,
        out_specs=tuple([hbm] * 9),
        scratch_shapes=[pltpu.SemaphoreType.DMA((9,))],
        compiler_params=pltpu.CompilerParams(vmem_limit_bytes=4 * 1024 * 1024),
    )(*results)
    results = list(results)
    results[6] = results[6].T
    results[7] = results[7].reshape(channels)
    return tuple(results)


def solution(mesh, x_count=X_CHIPS):
    placed = (
        P("chan", "ctx"),
        P("chan", "ctx"),
        P("chan", "ctx"),
        P("chan", "ctx"),
        P(None, "ctx"),
        P(),
        P(),
        P(None, "chan"),
        P("chan"),
        P("chan"),
    )
    return jax.shard_map(
        functools.partial(shards, x_count),
        mesh=mesh,
        in_specs=placed,
        out_specs=(
            P("chan", "ctx"),
            P("chan", "ctx"),
            P("chan", "ctx"),
            P("chan", "ctx"),
            P(),
            P(),
            P(None, "chan"),
            P("chan"),
            P(None, "ctx"),
        ),
        check_vma=False,
    )
```
